512 devices in a mesh: gx: 32 (over y, x, core), gy: 16 (over z).
Axes of the slice: x: 4, y: 4, z: 16, core: 2. Of those that a mesh axis runs over, the one named last changes fastest.
Arguments:
- initial: float32 [512, 1024, 128], P('gx', 'gy'), may hold values from -6 to 6, as said below
- material: int32 [512, 1024, 128], P('gx', 'gy'), may hold values from 0 to 7
- goal_faces: int32 [512, 1024, 128], P('gx', 'gy'), may hold values 0 or 1
- conductivity: float32 [8], replicated, may hold values from 0.2 to 2
Outputs:
- indicators: float32 [512, 1024, 128], P('gx', 'gy')
- sensitivity: float32 [512, 1024, 128], P('gx', 'gy')
The draws below stay inside these ranges and needn't reach their ends.
Inputs may be any that keep to these rules, and one draw needn't show every extreme that they name: `initial`: temperatures.
All inputs are finite; a program needn't handle non-finite values. No bound on the sum of `goal_faces` on one device may be relied on, other than what follows from the above.
Results may differ from the reference program's by a relative error of at most 0.00002.
Values sent between devices are 32-bit elements; how exact they have to be, the bound alone decides.
A program may use at most 64 MiB of HBM per device.

```python
import math
import jax
import jax.numpy as jnp

NZ = 128
STEPS = 3
MATS = 8
NX = 512
NY = 1024


def draw_initial(key, part):
    return jnp.clip(jax.random.normal(key, (NX, NY, NZ), jnp.float32), -6.0, 6.0)


def touch_ends(array, own_key, low, high):
    extent = array.shape
    index_at = [jax.random.randint(jax.random.fold_in(own_key, axis), (), 0, extent[axis]) for axis in range(len(extent))]
    array = array.at[tuple(index_at)].set(low)
    longest = extent.index(max(extent))
    index_at[longest] = (index_at[longest] + 1) % extent[longest]
    return array.at[tuple(index_at)].set(high)


def setup_inputs(seed: int = 0) -> dict:
    streams_of = jax.random.split(jax.random.key(seed), 5)
    initial = draw_initial(jax.random.fold_in(streams_of[4], 71), 0)
    material = touch_ends(jax.random.randint(streams_of[1], (NX, NY, NZ), 0, MATS), jax.random.fold_in(streams_of[1], 1), 0, MATS - 1).astype(jnp.int32)
    goal_faces = touch_ends((jax.random.randint(streams_of[2], (NX, NY, NZ), 0, 4) < 1).astype(jnp.int32), jax.random.fold_in(streams_of[2], 1), 0, 1)
    conductivity = jnp.clip(jnp.exp(jax.random.uniform(streams_of[3], (MATS,), jnp.float32, math.log(0.2), math.log(2.0))), 0.2, 2.0)
    return {"initial": initial, "material": material, "goal_faces": goal_faces, "conductivity": conductivity}


step_size = 0.075


def lookup(material, conductivity):
    result = jnp.zeros(material.shape, jnp.float32)
    for which in range(MATS):
        result = jnp.where(material == which, conductivity[which], result)
    return result


def neighbours(padded):
    return [padded[2:, 1:-1, 1:-1], padded[:-2, 1:-1, 1:-1], padded[1:-1, 2:, 1:-1],
            padded[1:-1, :-2, 1:-1], padded[1:-1, 1:-1, 2:], padded[1:-1, 1:-1, :-2]]


def face_values(padded):
    centre = padded[1:-1, 1:-1, 1:-1]
    return [0.5 * (centre + other) for other in neighbours(padded)]


def divergence(field, padded, weights):
    total = jnp.zeros_like(field)
    for weight, other in zip(weights, neighbours(padded)):
        total = total + weight * (other - field)
    return total


def patch_mean(padded):
    rows = padded[:-2] + padded[1:-1] + padded[2:]
    rows = rows[:, :-2] + rows[:, 1:-1] + rows[:, 2:]
    rows = rows[:, :, :-2] + rows[:, :, 1:-1] + rows[:, :, 2:]
    return rows / 27.0


def reference(initial, material, goal_faces, conductivity):
    conduct = lookup(material, conductivity)
    weights = face_values(jnp.pad(conduct, 1))
    states = [initial]
    slopes = []
    for section in range(STEPS):
        slopes.append(divergence(states[-1], jnp.pad(states[-1], 1), weights))
        states.append(states[-1] + step_size * slopes[-1])
    slopes.append(divergence(states[-1], jnp.pad(states[-1], 1), weights))
    residuals = [(states[section + 1] - states[section]) / step_size - slopes[section + 1] for section in range(STEPS)]
    flux = goal_faces.astype(jnp.float32) * weights[0]
    adjoint = flux - jnp.pad(flux, ((1, 0), (0, 0), (0, 0)))[:-1]
    indicators = jnp.zeros_like(initial)
    for section in range(STEPS - 1, -1, -1):
        padded = jnp.pad(adjoint, 1)
        indicators = indicators + residuals[section] * (patch_mean(padded) - adjoint)
        adjoint = adjoint + step_size * divergence(adjoint, padded, weights)
    return indicators, adjoint
```

```python
import functools

import jax
import jax.numpy as jnp
from jax import lax
from jax.experimental import pallas as pl
from jax.experimental.pallas import tpu as pltpu
from jax.sharding import PartitionSpec as P

MESH = pl.DeviceIdType.MESH
step_size = 0.075
HALO = 4
R0 = 8


def kernel(
    nx, ny, cond_in,
    u_in, m_in, g_in, u_rows, m_rows, g_rows,
    ind_out, sens_out,
    u_own, m_own, g_own, xu, xm, xg, yu, ym, yg, cu, cm, cg,
    K, WX, WY, WZ, C, G, V0, V1, V2, V3, Z3, Z2, Z1, T,
    cond, load_sem, x_send, x_recv, y_send, y_recv, c_send, c_recv,
):
    depth, rows, lanes = u_in.shape
    planes = depth + 2 * HALO
    ext = rows + 2 * HALO
    own0 = R0 + HALO
    gx, gy = lax.axis_index("gx"), lax.axis_index("gy")
    has_left, has_right = gx > 0, gx < nx - 1
    has_down, has_up = gy > 0, gy < ny - 1
    left, right = (gx - 1, gy), (gx + 1, gy)
    down, up = (gx, gy - 1), (gx, gy + 1)

    loads = [
        pltpu.make_async_copy(src, dst, load_sem.at[i])
        for i, (src, dst) in enumerate(((u_in, u_own), (m_in, m_own), (g_in, g_own), (cond_in, cond)))
    ]
    for load in loads:
        load.start()

    barrier = pltpu.get_barrier_semaphore()
    sides = ((has_left, left), (has_right, right), (has_down, down), (has_up, up))
    for there, who in sides:
        @pl.when(there)
        def _():
            pl.semaphore_signal(barrier, inc=1, device_id=who, device_id_type=MESH)
    pl.semaphore_wait(barrier, sum(there.astype(jnp.int32) for there, _ in sides))

    ins = (u_in, m_in, g_in)
    in_rows = (u_rows, m_rows, g_rows)
    xs, ys, cs = (xu, xm, xg), (yu, ym, yg), (cu, cm, cg)

    def remote(src, dst, send, recv, who):
        return pltpu.make_async_remote_copy(
            src_ref=src, dst_ref=dst, send_sem=send, recv_sem=recv,
            device_id=who, device_id_type=MESH,
        )

    def y_copy(side, a):
        who = up if side == 0 else down
        group = in_rows[a].shape[1] - 1 if side == 0 else 0
        return remote(in_rows[a].at[:, group], ys[a].at[side],
                      y_send.at[side, a], y_recv.at[side, a], who)

    def x_copy(side, j, a):
        who = right if side == 0 else left
        plane = depth - HALO + j if side == 0 else j
        return remote(ins[a].at[plane], xs[a].at[side, j],
                      x_send.at[side, j, a], x_recv.at[side, j, a], who)

    def c_copy(side, y_side, a):
        who = right if side == 0 else left
        first = depth - HALO if side == 0 else 0
        return remote(ys[a].at[y_side, pl.ds(first, HALO)], cs[a].at[side, y_side],
                      c_send.at[side, y_side, a], c_recv.at[side, y_side, a], who)

    sends_to = ((has_right, has_left), (has_up, has_down))
    comes_from = ((has_left, has_right), (has_down, has_up))

    def x_parts(side):
        order = (3, 2, 1, 0) if side == 0 else (0, 1, 2, 3)
        return [(j, a) for j in order for a in range(3) if not (side == 1 and j == 3 and a == 2)]

    for side in range(2):
        @pl.when(sends_to[1][side])
        def _():
            for a in range(3):
                y_copy(side, a).start()
        @pl.when(sends_to[0][side])
        def _():
            for j, a in x_parts(side):
                x_copy(side, j, a).start()

    for load in loads:
        load.wait()

    scale = 0.5 * step_size
    table = [cond[i] * scale for i in range(cond.shape[0])]

    def lookup(m):
        k = jnp.full(m.shape, table[0], jnp.float32)
        for i in range(1, len(table)):
            k = jnp.where(m == i, table[i], k)
        return k

    def fill(p, r, n, uv, mv, gv):
        V0[p, pl.ds(r, n), :] = uv
        K[p, pl.ds(r, n), :] = lookup(mv)
        G[p, pl.ds(r, n), :] = gv.astype(jnp.float32)

    def blank(p, r, n):
        zero = jnp.zeros((n, lanes), jnp.float32)
        for ref in (V0, K, G):
            ref[p, pl.ds(r, n), :] = zero

    @pl.loop(0, depth)
    def _(p):
        fill(p + HALO, own0, rows, u_own[p], m_own[p], g_own[p])

    for side in range(2):
        r = R0 if side == 0 else own0 + rows
        @pl.when(comes_from[1][side])
        def _():
            for a in range(3):
                y_copy(side, a).wait_recv()
            for x_side in range(2):
                @pl.when(sends_to[0][x_side])
                def _():
                    for a in range(3):
                        c_copy(x_side, side, a).start()

            @pl.loop(0, depth)
            def _(p):
                fill(p + HALO, r, HALO, yu[side, p], ym[side, p], yg[side, p])
        @pl.when(jnp.logical_not(comes_from[1][side]))
        def _():
            @pl.loop(0, planes)
            def _(p):
                blank(p, r, HALO)

    for side in range(2):
        base = 0 if side == 0 else depth + HALO
        @pl.when(comes_from[0][side])
        def _():
            for j, a in x_parts(side):
                x_copy(side, j, a).wait_recv()

            @pl.loop(0, HALO)
            def _(j):
                fill(base + j, own0, rows, xu[side, j], xm[side, j], xg[side, j])

            for y_side in range(2):
                r = R0 if y_side == 0 else own0 + rows
                @pl.when(comes_from[1][y_side])
                def _():
                    for a in range(3):
                        c_copy(side, y_side, a).wait_recv()

                    @pl.loop(0, HALO)
                    def _(j):
                        fill(base + j, r, HALO, cu[side, y_side, j], cm[side, y_side, j], cg[side, y_side, j])
        @pl.when(jnp.logical_not(comes_from[0][side]))
        def _():
            @pl.loop(0, HALO)
            def _(j):
                blank(base + j, R0, ext)
            near = HALO - 1 if side == 0 else HALO + depth
            zero = jnp.zeros((ext, lanes), jnp.float32)
            for ref in (V1, V2, V3, Z3, Z2, Z1):
                ref[near, pl.ds(R0, ext), :] = zero

    lane = lax.broadcasted_iota(jnp.int32, (ext, lanes), 1)
    row = lax.broadcasted_iota(jnp.int32, (ext, lanes), 0)
    inside = jnp.where(
        jnp.logical_and(
            jnp.logical_or(row >= HALO, has_down),
            jnp.logical_or(row < HALO + rows, has_up),
        ), 1.0, 0.0).astype(jnp.float32)
    mid, low, high = pl.ds(R0, ext), pl.ds(R0 - 1, ext), pl.ds(R0 + 1, ext)

    @pl.loop(0, planes - 1)
    def _(p):
        WX[p, mid, :] = K[p, mid, :] + K[p + 1, mid, :]

    @pl.loop(1, planes - 1)
    def _(p):
        k = K[p, mid, :]
        above = jnp.where(lane == lanes - 1, 0.0, pltpu.roll(k, lanes - 1, 1))
        below = jnp.where(lane == 0, 0.0, pltpu.roll(k, 1, 1))
        k2 = k + k
        WY[p, mid, :] = k + K[p, high, :]
        WZ[p, mid, :] = jnp.where(lane == lanes - 1, 0.0, k + above)
        C[p, mid, :] = (WX[p, mid, :] + WX[p - 1, mid, :] + (k2 + (K[p, low, :] + K[p, high, :]))
                        + (k2 + (above + below)))

    def spread(src, p):
        v = src[p, mid, :]
        wz = WZ[p, mid, :]
        return v, (
            (WX[p, mid, :] * src[p + 1, mid, :] + WX[p - 1, mid, :] * src[p - 1, mid, :])
            + (WY[p, mid, :] * src[p, high, :] + WY[p, low, :] * src[p, low, :])
            + (wz * pltpu.roll(v, lanes - 1, 1) + pltpu.roll(wz * v, 1, 1))
            - C[p, mid, :] * v
        )

    def bounds(n):
        return (jnp.where(has_left, n, HALO), jnp.where(has_right, planes - n, planes - HALO))

    first, last = bounds(1)

    @pl.loop(first, last)
    def _(p):
        Z3[p, mid, :] = inside * (G[p, mid, :] * WX[p, mid, :] - G[p - 1, mid, :] * WX[p - 1, mid, :])

    for n, (src, dst, zsrc, zdst) in enumerate(((V0, V1, None, None), (V1, V2, Z3, Z2), (V2, V3, Z2, Z1))):
        first, last = bounds(n + 1)

        @pl.loop(first, last)
        def _(p):
            dst[p, mid, :] = inside * spread(src, p)[1]
            if zsrc is not None:
                v, d = spread(zsrc, p)
                zdst[p, mid, :] = v + inside * d

    own = pl.ds(own0, rows)
    own_low, own_high = pl.ds(own0 - 1, rows), pl.ds(own0 + 1, rows)
    own_lane = lax.broadcasted_iota(jnp.int32, (rows, lanes), 1)

    @pl.loop(HALO, HALO + depth)
    def _(p):
        v, d = spread(Z1, p)
        T[3, mid, :] = v + d
        e3 = spread(V3, p)[1]
        T[4, mid, :] = e3
        for i, z in enumerate((Z1, Z2, Z3)):
            T[i, mid, :] = z[p - 1, mid, :] + z[p, mid, :] + z[p + 1, mid, :]
        q = []
        for i, z in enumerate((Z1, Z2, Z3)):
            s = T[i, own_low, :] + T[i, own, :] + T[i, own_high, :]
            s = s + jnp.where(own_lane == lanes - 1, 0.0, pltpu.roll(s, lanes - 1, 1)) + jnp.where(
                own_lane == 0, 0.0, pltpu.roll(s, 1, 1))
            q.append(s * (1.0 / 27.0) - z[p, own, :])
        e1, e2 = V2[p, own, :], V3[p, own, :]
        r1 = e1 + e2
        r2 = r1 + e2 + T[4, own, :]
        ind_out[p - HALO] = (e1 * q[0] + r1 * q[1] + r2 * q[2]) * (-1.0 / (step_size * step_size))
        sens_out[p - HALO] = T[3, own, :] * (1.0 / step_size)

    for side in range(2):
        @pl.when(sends_to[1][side])
        def _():
            for a in range(3):
                y_copy(side, a).wait_send()
        @pl.when(sends_to[0][side])
        def _():
            for j, a in x_parts(side):
                x_copy(side, j, a).wait_send()
            for y_side in range(2):
                @pl.when(comes_from[1][y_side])
                def _():
                    for a in range(3):
                        c_copy(side, y_side, a).wait_send()


def solution(mesh):
    nx, ny = mesh.shape["gx"], mesh.shape["gy"]

    def step(initial, material, goal_faces, conductivity):
        depth, rows, lanes = initial.shape
        planes, tall = depth + 2 * HALO, rows + 2 * HALO + 16
        f32, i32 = jnp.float32, jnp.int32
        by_rows = (depth, rows // HALO, HALO, lanes)
        halos = []
        for shape in ((2, HALO, rows, lanes), (2, depth, HALO, lanes), (2, 2, HALO, HALO, lanes)):
            halos += [pltpu.VMEM(shape, t) for t in (f32, i32, i32)]
        sem = pltpu.SemaphoreType.DMA
        whole = pl.BlockSpec(memory_space=pltpu.MemorySpace.HBM)
        inside = pl.BlockSpec(memory_space=pltpu.VMEM)
        return pl.pallas_call(
            functools.partial(kernel, nx, ny),
            out_shape=[jax.ShapeDtypeStruct(initial.shape, f32)] * 2,
            in_specs=[whole] * 7,
            out_specs=[inside, inside],
            scratch_shapes=[pltpu.VMEM((depth, rows, lanes), t) for t in (f32, i32, i32)]
            + halos
            + [pltpu.VMEM((planes, tall, lanes), f32) for _ in range(13)]
            + [pltpu.VMEM((5, tall, lanes), f32)]
            + [pltpu.SMEM(conductivity.shape, f32), sem((4,)), sem((2, HALO, 3)), sem((2, HALO, 3)), sem((2, 3)), sem((2, 3)),
               sem((2, 2, 3)), sem((2, 2, 3))],
            compiler_params=pltpu.CompilerParams(collective_id=0, has_side_effects=True),
        )(conductivity, initial, material, goal_faces,
          initial.reshape(by_rows), material.reshape(by_rows), goal_faces.reshape(by_rows))

    placed = P("gx", "gy", None)
    return jax.shard_map(
        step,
        mesh=mesh,
        in_specs=(placed, placed, placed, P()),
        out_specs=(placed, placed),
        check_vma=False,
    )
```

```python
import functools

import jax
import jax.numpy as jnp
from jax import lax
from jax.experimental import pallas as pl
from jax.experimental.pallas import tpu as pltpu
from jax.sharding import PartitionSpec as P

MESH = pl.DeviceIdType.MESH
step_size = 0.075
HALO = 4
R0 = 8
CHUNK = 8


def kernel(
    nx, ny, cond_in,
    u_in, m_in, g_in, u_rows, m_rows, g_rows,
    ind_out, sens_out,
    u_own, m_own, g_own, xu, xm, xg, yu, ym, yg, cu, cm, cg,
    K, WX, WY, WZ, WB, C, G, V0, V1, V2, V3, Z3, Z2, Z1, S3, S2, M, T,
    cond, load_sem, x_send, x_recv, y_send, y_recv, c_send, c_recv,
):
    depth, rows, lanes = u_in.shape
    planes = depth + 2 * HALO
    ext = rows + 2 * HALO
    own0 = R0 + HALO
    gx, gy = lax.axis_index("gx"), lax.axis_index("gy")
    has_left, has_right = gx > 0, gx < nx - 1
    has_down, has_up = gy > 0, gy < ny - 1
    left, right = (gx - 1, gy), (gx + 1, gy)
    down, up = (gx, gy - 1), (gx, gy + 1)
    odd = lax.rem(gx, 2)

    barrier = pltpu.get_barrier_semaphore()
    sides = ((has_left, left), (has_right, right), (has_down, down), (has_up, up))
    for there, who in sides:
        @pl.when(there)
        def _():
            pl.semaphore_signal(barrier, inc=1, device_id=who, device_id_type=MESH)

    loads = [
        pltpu.make_async_copy(src, dst, load_sem.at[i])
        for i, (src, dst) in enumerate(((cond_in, cond), (m_in, m_own), (u_in, u_own), (g_in, g_own)))
    ]
    for load in loads:
        load.start()

    ins = (u_in, m_in, g_in)
    in_rows = (u_rows, m_rows, g_rows)
    xs, ys, cs = (xu, xm, xg), (yu, ym, yg), (cu, cm, cg)

    def remote(src, dst, send, recv, who):
        return pltpu.make_async_remote_copy(
            src_ref=src, dst_ref=dst, send_sem=send, recv_sem=recv,
            device_id=who, device_id_type=MESH,
        )

    def y_copy(side, a):
        who = up if side == 0 else down
        group = in_rows[a].shape[1] - 1 if side == 0 else 0
        return remote(in_rows[a].at[:, group], ys[a].at[side],
                      y_send.at[side, a], y_recv.at[side, a], who)

    def x_copy(side, j, a):
        who = right if side == 0 else left
        plane = depth - HALO + j if side == 0 else j
        return remote(ins[a].at[plane], xs[a].at[side, j],
                      x_send.at[side, j, a], x_recv.at[side, j, a], who)

    def c_copy(side, y_side, a):
        who = right if side == 0 else left
        first = depth - HALO if side == 0 else 0
        return remote(ys[a].at[y_side, pl.ds(first, HALO)], cs[a].at[side, y_side],
                      c_send.at[side, y_side, a], c_recv.at[side, y_side, a], who)

    sends_to = ((has_right, has_left), (has_up, has_down))
    comes_from = ((has_left, has_right), (has_down, has_up))

    def x_parts(side):
        order = (3, 2, 1, 0) if side == 0 else (0, 1, 2, 3)
        return [(j, a) for j in order for a in (1, 0, 2) if not (side == 1 and j == 3 and a == 2)]

    def lane_is(which, n):
        return lax.broadcasted_iota(jnp.int32, (n, lanes), 1) == which

    def turned(v):
        return pltpu.roll(v, lanes - 1, 1), pltpu.roll(v, 1, 1)

    def ends_off(a, b):
        n = a.shape[0]
        return jnp.where(lane_is(lanes - 1, n), 0.0, a), jnp.where(lane_is(0, n), 0.0, b)

    def chunks(r, n):
        while n > 0:
            yield r, min(n, CHUNK)
            r, n = r + CHUNK, n - CHUNK

    def fill(p, r, n, read):
        for i in range(0, n, CHUNK):
            m = min(CHUNK, n - i)
            uv, mv, gv = read(i, m)
            at = pl.ds(r + i, m)
            k = jnp.full(mv.shape, table[0], jnp.float32)
            for w in range(1, len(table)):
                k = jnp.where(mv == w, table[w], k)
            K[p, at, :] = k
            V0[p, at, :] = uv
            G[p, at, :] = gv.astype(jnp.float32)

    def blank(p, r, n):
        zero = jnp.zeros((n, lanes), jnp.float32)
        for ref in (V0, K, G):
            ref[p, pl.ds(r, n), :] = zero

    def faces_x(p, r, n):
        for s, m in chunks(r, n):
            at = pl.ds(s, m)
            WX[p, at, :] = K[p, at, :] + K[p + 1, at, :]

    def faces(p, r, n):
        for s, m in chunks(r, n):
            at, lo, hi = pl.ds(s, m), pl.ds(s - 1, m), pl.ds(s + 1, m)
            k = K[p, at, :]
            a, b = ends_off(*turned(k))
            h = K[p, hi, :]
            k2 = k + k
            WY[p, at, :] = k + h
            WZ[p, at, :] = jnp.where(lane_is(lanes - 1, m), 0.0, k + a)
            WB[p, at, :] = jnp.where(lane_is(0, m), 0.0, k + b)
            C[p, at, :] = ((WX[p, at, :] + WX[p - 1, at, :]) + (k2 + (K[p, lo, :] + h))) + (k2 + (a + b))

    def start_z(p, r, n, mask=None):
        for s, m in chunks(r, n):
            at = pl.ds(s, m)
            z = G[p, at, :] * WX[p, at, :] - G[p - 1, at, :] * WX[p - 1, at, :]
            Z3[p, at, :] = z if mask is None else z * mask(s, m)

    def spread(src, p, s, m):
        at, lo, hi = pl.ds(s, m), pl.ds(s - 1, m), pl.ds(s + 1, m)
        v = src[p, at, :]
        a, b = turned(v)
        d = (
            (WX[p, at, :] * src[p + 1, at, :] + WX[p - 1, at, :] * src[p - 1, at, :])
            + (WY[p, at, :] * src[p, hi, :] + WY[p, lo, :] * src[p, lo, :])
            + (WZ[p, at, :] * a + WB[p, at, :] * b)
            - C[p, at, :] * v
        )
        return v, a, b, d

    def forward(n, p, r, k, mask=None):
        src, dst = ((V0, V1), (V1, V2), (V2, V3))[n]
        for s, m in chunks(r, k):
            d = spread(src, p, s, m)[3]
            dst[p, pl.ds(s, m), :] = d if mask is None else d * mask(s, m)

    def backward(n, p, r, k, mask=None):
        src, dst, box = (None, (Z3, Z2, S3), (Z2, Z1, S2))[n]
        for s, m in chunks(r, k):
            v, a, b, d = spread(src, p, s, m)
            at = pl.ds(s, m)
            dst[p, at, :] = v + (d if mask is None else d * mask(s, m))
            a, b = ends_off(a, b)
            box[p, at, :] = v + (a + b)

    def finish(p):
        for i, z in enumerate((Z1, S2, S3)):
            for s, m in chunks(own0 - 1, rows + 2):
                at = pl.ds(s, m)
                T[i, at, :] = z[p - 1, at, :] + z[p, at, :] + z[p + 1, at, :]
        for s, m in chunks(own0, rows):
            at, lo, hi = pl.ds(s, m), pl.ds(s - 1, m), pl.ds(s + 1, m)
            e1, e2, e3 = V2[p, at, :], V3[p, at, :], spread(V3, p, s, m)[3]
            z1, _, _, d = spread(Z1, p, s, m)
            r1 = e1 + e2
            r2 = r1 + (e2 + e3)
            sums = [T[i, lo, :] + T[i, at, :] + T[i, hi, :] for i in range(3)]
            a, b = ends_off(*turned(sums[0]))
            q1 = sums[0] + (a + b)
            third = 1.0 / 27.0
            total = (e1 * (q1 * third - z1) + r1 * (sums[1] * third - Z2[p, at, :])
                     + r2 * (sums[2] * third - Z3[p, at, :]))
            out = pl.ds(s - own0, m)
            ind_out[p - HALO, out, :] = total * (-1.0 / (step_size * step_size))
            sens_out[p - HALO, out, :] = (z1 + d) * (1.0 / step_size)

    loads[0].wait()
    loads[1].wait()
    loads[2].wait()
    loads[3].wait()
    table = [cond[i] * (0.5 * step_size) for i in range(cond.shape[0])]
    row = lax.broadcasted_iota(jnp.int32, (ext, lanes), 0)
    M[pl.ds(R0, ext), :] = jnp.where(
        jnp.logical_and(
            jnp.logical_or(row >= HALO, has_down),
            jnp.logical_or(row < HALO + rows, has_up),
        ), 1.0, 0.0).astype(jnp.float32)

    pl.semaphore_wait(barrier, sum(there.astype(jnp.int32) for there, _ in sides))
    for side in range(2):
        @pl.when(sends_to[1][side])
        def _():
            for a in range(3):
                y_copy(side, a).start()
    for side in range(2):
        @pl.when(sends_to[0][side])
        def _():
            for j, a in x_parts(side):
                x_copy(side, j, a).start()

    @pl.loop(0, depth)
    def _(p):
        fill(p + HALO, own0, rows, lambda i, m: (
            u_own[p, pl.ds(i, m), :], m_own[p, pl.ds(i, m), :], g_own[p, pl.ds(i, m), :]))

    first, last = HALO + 1, HALO + depth - 1

    def each(lo, hi, body, unroll=2):
        @pl.loop(0, (hi - lo) // unroll)
        def _(i):
            for j in range(unroll):
                body(lo + i * unroll + j)

    @pl.loop(HALO, last)
    def _(p):
        faces_x(p, own0, rows)

    each(first, last, lambda p: (faces(p, own0, rows), start_z(p, own0, rows)))
    for n in range(3):
        def inner(p):
            forward(n, p, own0 + 1 + n, rows - 2 - 2 * n)
            if n:
                backward(n, p, own0 + 1 + n, rows - 2 - 2 * n)
        each(first + n, last - n, inner)

    for side in range(2):
        r = R0 if side == 0 else own0 + rows
        @pl.when(comes_from[1][side])
        def _():
            for a in range(3):
                y_copy(side, a).wait_recv()
            for x_side in range(2):
                @pl.when(sends_to[0][x_side])
                def _():
                    for a in range(3):
                        c_copy(x_side, side, a).start()

            @pl.loop(0, depth)
            def _(p):
                fill(p + HALO, r, HALO, lambda i, m: (yu[side, p], ym[side, p], yg[side, p]))
        @pl.when(jnp.logical_not(comes_from[1][side]))
        def _():
            @pl.loop(0, planes)
            def _(p):
                blank(p, r, HALO)

    def row_mask(s, m):
        return M[pl.ds(s, m), :]

    edge_tiles = (R0, own0 + rows - HALO)

    @pl.loop(HALO, last)
    def _(p):
        for r in edge_tiles:
            faces_x(p, r, 2 * HALO)

    def edges(p):
        for r in edge_tiles:
            faces(p, r, 2 * HALO)
            start_z(p, r, 2 * HALO, row_mask)
    each(first, last, edges)
    for n in range(3):
        def strip(p):
            for r in (R0 + 1 + n, own0 + rows - 1 - n):
                forward(n, p, r, HALO, row_mask)
                if n:
                    backward(n, p, r, HALO, row_mask)
        each(first + n, last - n, strip)
    each(2 * HALO, depth, finish, 1)

    @pl.loop(0, 2)
    def _(turn):
        high = lax.rem(odd + 1 + turn, 2)
        base = high * (depth + HALO)
        for side in range(2):
            @pl.when(high == side)
            def _():
                @pl.when(comes_from[0][side])
                def _():
                    for j, a in x_parts(side):
                        x_copy(side, j, a).wait_recv()
                    for y_side in range(2):
                        @pl.when(comes_from[1][y_side])
                        def _():
                            for a in range(3):
                                c_copy(side, y_side, a).wait_recv()

        there = jnp.where(high == 1, has_right, has_left)

        @pl.when(there)
        def _():
            @pl.loop(0, HALO)
            def _(j):
                fill(base + j, own0, rows, lambda i, m: (
                    xu[high, j, pl.ds(i, m), :], xm[high, j, pl.ds(i, m), :], xg[high, j, pl.ds(i, m), :]))
                for y_side in range(2):
                    @pl.when(comes_from[1][y_side])
                    def _():
                        fill(base + j, R0 if y_side == 0 else own0 + rows, HALO, lambda i, m: (
                            cu[high, y_side, j], cm[high, y_side, j], cg[high, y_side, j]))

        @pl.when(jnp.logical_not(there))
        def _():
            @pl.loop(0, HALO)
            def _(j):
                blank(base + j, R0, ext)

        @pl.loop(0, HALO)
        def _(j):
            faces_x(high * (depth + HALO - 1) + j, R0, ext)

        def plane_mask(p):
            inside = jnp.logical_or(there, jnp.logical_and(p >= HALO, p < HALO + depth))
            scale = jnp.where(inside, 1.0, 0.0).astype(jnp.float32)
            return lambda s, m: M[pl.ds(s, m), :] * scale

        def start(p):
            faces(p, R0, ext)
            start_z(p, R0, ext, plane_mask(p))

        lo = 1 + high * (depth + 2)
        each(lo, lo + HALO, start)
        for n in range(3):
            def shell(p):
                forward(n, p, R0 + 1 + n, ext - 2 - 2 * n, plane_mask(p))
                if n:
                    backward(n, p, R0 + 1 + n, ext - 2 - 2 * n, plane_mask(p))
            begin = lo + n - 2 * n * high
            each(begin, begin + HALO, shell)
        begin = HALO + high * (depth - HALO)
        each(begin, begin + HALO, finish, 1)

    for side in range(2):
        @pl.when(sends_to[1][side])
        def _():
            for a in range(3):
                y_copy(side, a).wait_send()
        @pl.when(sends_to[0][side])
        def _():
            for j, a in x_parts(side):
                x_copy(side, j, a).wait_send()
            for y_side in range(2):
                @pl.when(comes_from[1][y_side])
                def _():
                    for a in range(3):
                        c_copy(side, y_side, a).wait_send()


def put_out(a, b, a_out, b_out, sem):
    part = a.shape[0] // 4
    copies = [
        pltpu.make_async_copy(src.at[pl.ds(q * part, part)], dst.at[pl.ds(q * part, part)], sem.at[i, q])
        for i, (src, dst) in enumerate(((a, a_out), (b, b_out))) for q in range(4)
    ]
    for copy in copies:
        copy.start()
    for copy in copies:
        copy.wait()


def solution(mesh):
    nx, ny = mesh.shape["gx"], mesh.shape["gy"]

    def step(initial, material, goal_faces, conductivity):
        depth, rows, lanes = initial.shape
        planes, tall = depth + 2 * HALO, rows + 2 * HALO + 16
        f32, i32 = jnp.float32, jnp.int32
        by_rows = (depth, rows // HALO, HALO, lanes)
        halos = []
        for shape in ((2, HALO, rows, lanes), (2, depth, HALO, lanes), (2, 2, HALO, HALO, lanes)):
            halos += [pltpu.VMEM(shape, t) for t in (f32, i32, i32)]
        sem = pltpu.SemaphoreType.DMA
        whole = pl.BlockSpec(memory_space=pltpu.MemorySpace.HBM)
        inside = pl.BlockSpec(memory_space=pltpu.VMEM)

        def keep(v):
            return pltpu.with_memory_space_constraint(v, pltpu.MemorySpace.HBM)

        args = (conductivity, initial, material, goal_faces,
                initial.reshape(by_rows), material.reshape(by_rows), goal_faces.reshape(by_rows))
        ind, sens = pl.pallas_call(
            functools.partial(kernel, nx, ny),
            out_shape=[pltpu.VMEM(initial.shape, f32)] * 2,
            in_specs=[whole] * 7,
            out_specs=[inside, inside],
            scratch_shapes=[pltpu.VMEM((depth, rows, lanes), t) for t in (f32, i32, i32)]
            + halos
            + [pltpu.VMEM((planes, tall, lanes), f32) for _ in range(16)]
            + [pltpu.VMEM((tall, lanes), f32), pltpu.VMEM((3, tall, lanes), f32)]
            + [pltpu.SMEM(conductivity.shape, f32), sem((4,)), sem((2, HALO, 3)), sem((2, HALO, 3)),
               sem((2, 3)), sem((2, 3)), sem((2, 2, 3)), sem((2, 2, 3))],
            compiler_params=pltpu.CompilerParams(
                collective_id=0, has_side_effects=True, vmem_limit_bytes=50 << 20),
            name="cells",
        )(*(keep(v) for v in args))
        return pl.pallas_call(
            put_out,
            out_shape=[jax.ShapeDtypeStruct(initial.shape, f32)] * 2,
            in_specs=[inside] * 2,
            out_specs=[pl.BlockSpec(memory_space=pl.ANY)] * 2,
            scratch_shapes=[sem((2, 4))],
            compiler_params=pltpu.CompilerParams(vmem_limit_bytes=4 << 20),
            name="put_out",
        )(ind, sens)

    placed = P("gx", "gy", None)
    return jax.shard_map(
        step,
        mesh=mesh,
        in_specs=(placed, placed, placed, P()),
        out_specs=(placed, placed),
        check_vma=False,
    )
```

```python
import functools

import jax
import jax.numpy as jnp
from jax import lax
from jax.experimental import pallas as pl
from jax.experimental.pallas import tpu as pltpu
from jax.sharding import PartitionSpec as P

MESH = pl.DeviceIdType.MESH
step_size = 0.075
HALO = 4
R0 = 8
CHUNK = 8


def kernel(
    nx, ny, cond_in,
    u_in, m_in, g_in, u_rows, m_rows, g_rows,
    ind_out, sens_out,
    u_own, m_own, g_own, xu, xm, xg, yu, ym, yg, cu, cm, cg, eu, em, eg,
    K, WX, WY, WZ, WB, C, G, V0, V1, V2, V3, Z3, Z2, Z1, S3, S2, M, T,
    cond, load_sem, x_send, x_recv, y_send, y_recv, c_send, c_recv, e_send, e_recv, late,
):
    depth, rows, lanes = u_in.shape
    planes = depth + 2 * HALO
    ext = rows + 2 * HALO
    own0 = R0 + HALO
    gx, gy = lax.axis_index("gx"), lax.axis_index("gy")
    has_left, has_right = gx > 0, gx < nx - 1
    has_down, has_up = gy > 0, gy < ny - 1
    left, right = (gx - 1, gy), (gx + 1, gy)
    down, up = (gx, gy - 1), (gx, gy + 1)
    odd = lax.rem(gx, 2)

    both, either = jnp.logical_and, jnp.logical_or
    is_first = both(gx == 0, gy == 0)
    beside_x, beside_y = both(gx == 1, gy == 0), both(gx == 0, gy == 1)
    across = both(gx == 1, gy == 1)
    beside = either(beside_x, beside_y)

    def unless(cond, but):
        return both(cond, jnp.logical_not(but))

    barrier = pltpu.get_barrier_semaphore()
    sides = ((has_left, left), (has_right, right), (has_down, down), (has_up, up))
    for there, who in sides:
        @pl.when(unless(there, is_first))
        def _():
            pl.semaphore_signal(barrier, inc=1, device_id=who, device_id_type=MESH)

    loads = [
        pltpu.make_async_copy(src, dst, load_sem.at[i])
        for i, (src, dst) in enumerate(((cond_in, cond), (m_in, m_own), (u_in, u_own), (g_in, g_own)))
    ]
    for load in loads:
        load.start()

    ins = (u_in, m_in, g_in)
    in_rows = (u_rows, m_rows, g_rows)
    xs, ys, cs = (xu, xm, xg), (yu, ym, yg), (cu, cm, cg)

    def remote(src, dst, send, recv, who):
        return pltpu.make_async_remote_copy(
            src_ref=src, dst_ref=dst, send_sem=send, recv_sem=recv,
            device_id=who, device_id_type=MESH,
        )

    y_parts = ((0, HALO), (depth - HALO, HALO), (HALO, depth - 2 * HALO))

    def y_copy(side, part, a):
        who = up if side == 0 else down
        group = in_rows[a].shape[1] - 1 if side == 0 else 0
        at = pl.ds(*y_parts[part])
        return remote(in_rows[a].at[at, group], ys[a].at[side, at],
                      y_send.at[side, part, a], y_recv.at[side, part, a], who)

    def y_start(side):
        for part in range(3):
            for a in range(3):
                y_copy(side, part, a).start()

    def x_start(side):
        for j, a in x_parts(side):
            x_copy(side, j, a).start()

    def x_copy(side, j, a):
        who = right if side == 0 else left
        plane = depth - HALO + j if side == 0 else j
        return remote(ins[a].at[plane], xs[a].at[side, j],
                      x_send.at[side, j, a], x_recv.at[side, j, a], who)

    def c_copy(side, y_side, a):
        who = right if side == 0 else left
        first = depth - HALO if side == 0 else 0
        return remote(ys[a].at[y_side, pl.ds(first, HALO)], cs[a].at[side, y_side],
                      c_send.at[side, y_side, a], c_recv.at[side, y_side, a], who)

    def e_copy(a):
        return remote(xs[a].at[0, :, pl.ds(0, 2 * HALO)], (eu, em, eg)[a],
                      e_send.at[a], e_recv.at[a], down)

    sends_to = ((has_right, has_left), (has_up, has_down))
    comes_from = ((has_left, has_right), (has_down, has_up))

    def c_sent(x_side, y_side):
        there = sends_to[0][x_side]
        return unless(there, is_first) if (x_side, y_side) == (0, 1) else there

    def c_now(x_side, y_side):
        there = c_sent(x_side, y_side)
        return unless(there, beside_x) if x_side == 1 else there

    def x_parts(side):
        order = (3, 2, 1, 0) if side == 0 else (0, 1, 2, 3)
        return [(j, a) for j in order for a in (1, 0, 2) if not (side == 1 and j == 3 and a == 2)]

    def lane_is(which, n):
        return lax.broadcasted_iota(jnp.int32, (n, lanes), 1) == which

    def turned(v):
        return pltpu.roll(v, lanes - 1, 1), pltpu.roll(v, 1, 1)

    def ends_off(a, b):
        n = a.shape[0]
        return jnp.where(lane_is(lanes - 1, n), 0.0, a), jnp.where(lane_is(0, n), 0.0, b)

    def chunks(r, n):
        while n > 0:
            yield r, min(n, CHUNK)
            r, n = r + CHUNK, n - CHUNK

    def fill(p, r, n, read):
        for i in range(0, n, CHUNK):
            m = min(CHUNK, n - i)
            uv, mv, gv = read(i, m)
            at = pl.ds(r + i, m)
            k = jnp.full(mv.shape, table[0], jnp.float32)
            for w in range(1, len(table)):
                k = jnp.where(mv == w, table[w], k)
            K[p, at, :] = k
            V0[p, at, :] = uv
            G[p, at, :] = gv.astype(jnp.float32)

    def blank(p, r, n):
        zero = jnp.zeros((n, lanes), jnp.float32)
        for ref in (V0, K, G):
            ref[p, pl.ds(r, n), :] = zero

    def faces_x(p, r, n):
        for s, m in chunks(r, n):
            at = pl.ds(s, m)
            WX[p, at, :] = K[p, at, :] + K[p + 1, at, :]

    def faces(p, r, n):
        for s, m in chunks(r, n):
            at, lo, hi = pl.ds(s, m), pl.ds(s - 1, m), pl.ds(s + 1, m)
            k = K[p, at, :]
            a, b = ends_off(*turned(k))
            h = K[p, hi, :]
            k2 = k + k
            WY[p, at, :] = k + h
            WZ[p, at, :] = jnp.where(lane_is(lanes - 1, m), 0.0, k + a)
            WB[p, at, :] = jnp.where(lane_is(0, m), 0.0, k + b)
            C[p, at, :] = ((WX[p, at, :] + WX[p - 1, at, :]) + (k2 + (K[p, lo, :] + h))) + (k2 + (a + b))

    def start_z(p, r, n, mask=None):
        for s, m in chunks(r, n):
            at = pl.ds(s, m)
            z = G[p, at, :] * WX[p, at, :] - G[p - 1, at, :] * WX[p - 1, at, :]
            Z3[p, at, :] = z if mask is None else z * mask(s, m)

    def spread(src, p, s, m):
        at, lo, hi = pl.ds(s, m), pl.ds(s - 1, m), pl.ds(s + 1, m)
        v = src[p, at, :]
        a, b = turned(v)
        d = (
            (WX[p, at, :] * src[p + 1, at, :] + WX[p - 1, at, :] * src[p - 1, at, :])
            + (WY[p, at, :] * src[p, hi, :] + WY[p, lo, :] * src[p, lo, :])
            + (WZ[p, at, :] * a + WB[p, at, :] * b)
            - C[p, at, :] * v
        )
        return v, a, b, d

    def forward(n, p, r, k, mask=None):
        src, dst = ((V0, V1), (V1, V2), (V2, V3))[n]
        for s, m in chunks(r, k):
            d = spread(src, p, s, m)[3]
            dst[p, pl.ds(s, m), :] = d if mask is None else d * mask(s, m)

    def backward(n, p, r, k, mask=None):
        src, dst, box = (None, (Z3, Z2, S3), (Z2, Z1, S2))[n]
        for s, m in chunks(r, k):
            v, a, b, d = spread(src, p, s, m)
            at = pl.ds(s, m)
            dst[p, at, :] = v + (d if mask is None else d * mask(s, m))
            a, b = ends_off(a, b)
            box[p, at, :] = v + (a + b)

    def finish(p):
        for i, z in enumerate((Z1, S2, S3)):
            for s, m in chunks(own0 - 1, rows + 2):
                at = pl.ds(s, m)
                T[i, at, :] = z[p - 1, at, :] + z[p, at, :] + z[p + 1, at, :]
        for s, m in chunks(own0, rows):
            at, lo, hi = pl.ds(s, m), pl.ds(s - 1, m), pl.ds(s + 1, m)
            e1, e2, e3 = V2[p, at, :], V3[p, at, :], spread(V3, p, s, m)[3]
            z1, _, _, d = spread(Z1, p, s, m)
            r1 = e1 + e2
            r2 = r1 + (e2 + e3)
            sums = [T[i, lo, :] + T[i, at, :] + T[i, hi, :] for i in range(3)]
            a, b = ends_off(*turned(sums[0]))
            q1 = sums[0] + (a + b)
            third = 1.0 / 27.0
            total = (e1 * (q1 * third - z1) + r1 * (sums[1] * third - Z2[p, at, :])
                     + r2 * (sums[2] * third - Z3[p, at, :]))
            out = pl.ds(s - own0, m)
            ind_out[p - HALO, out, :] = total * (-1.0 / (step_size * step_size))
            sens_out[p - HALO, out, :] = (z1 + d) * (1.0 / step_size)

    loads[0].wait()
    loads[1].wait()
    loads[2].wait()
    loads[3].wait()
    table = [cond[i] * (0.5 * step_size) for i in range(cond.shape[0])]
    row = lax.broadcasted_iota(jnp.int32, (ext, lanes), 0)
    M[pl.ds(R0, ext), :] = jnp.where(
        jnp.logical_and(
            jnp.logical_or(row >= HALO, has_down),
            jnp.logical_or(row < HALO + rows, has_up),
        ), 1.0, 0.0).astype(jnp.float32)

    pl.semaphore_wait(barrier, sum(there.astype(jnp.int32) for there, _ in sides) - beside.astype(jnp.int32))

    @pl.when(is_first)
    def _():
        for who in (right, up):
            pl.semaphore_signal(late, inc=1, device_id=who, device_id_type=MESH)

    for side in range(2):
        @pl.when(unless(sends_to[1][side], beside_y) if side else sends_to[1][side])
        def _():
            y_start(side)
    for side in range(2):
        @pl.when(unless(sends_to[0][side], beside_x) if side else sends_to[0][side])
        def _():
            x_start(side)

    @pl.loop(0, depth)
    def _(p):
        fill(p + HALO, own0, rows, lambda i, m: (
            u_own[p, pl.ds(i, m), :], m_own[p, pl.ds(i, m), :], g_own[p, pl.ds(i, m), :]))

    first, last = HALO + 1, HALO + depth - 1

    def each(lo, hi, body, unroll=2):
        @pl.loop(0, (hi - lo) // unroll)
        def _(i):
            for j in range(unroll):
                body(lo + i * unroll + j)

    @pl.loop(HALO, last)
    def _(p):
        faces_x(p, own0, rows)

    each(first, last, lambda p: (faces(p, own0, rows), start_z(p, own0, rows)))
    for n in range(3):
        def inner(p):
            forward(n, p, own0 + 1 + n, rows - 2 - 2 * n)
            if n:
                backward(n, p, own0 + 1 + n, rows - 2 - 2 * n)
        each(first + n, last - n, inner)

    @pl.when(beside_y)
    def _():
        pl.semaphore_wait(late, 1)
        y_start(1)

    @pl.when(across)
    def _():
        for j, a in x_parts(0):
            x_copy(0, j, a).wait_recv()
        for a in range(3):
            e_copy(a).start()

    for side in range(2):
        @pl.when(comes_from[1][side])
        def _():
            for part in range(2):
                for a in range(3):
                    y_copy(side, part, a).wait_recv()
            for x_side in range(2):
                @pl.when(c_now(x_side, side))
                def _():
                    for a in range(3):
                        c_copy(x_side, side, a).start()
    for side in range(2):
        r = R0 if side == 0 else own0 + rows
        @pl.when(comes_from[1][side])
        def _():
            for a in range(3):
                y_copy(side, 2, a).wait_recv()

            @pl.loop(0, depth)
            def _(p):
                fill(p + HALO, r, HALO, lambda i, m: (yu[side, p], ym[side, p], yg[side, p]))
        @pl.when(jnp.logical_not(comes_from[1][side]))
        def _():
            @pl.loop(0, planes)
            def _(p):
                blank(p, r, HALO)

    def row_mask(s, m):
        return M[pl.ds(s, m), :]

    edge_tiles = (R0, own0 + rows - HALO)

    @pl.loop(HALO, last)
    def _(p):
        for r in edge_tiles:
            faces_x(p, r, 2 * HALO)

    def edges(p):
        for r in edge_tiles:
            faces(p, r, 2 * HALO)
            start_z(p, r, 2 * HALO, row_mask)
    each(first, last, edges)
    for n in range(3):
        def strip(p):
            for r in (R0 + 1 + n, own0 + rows - 1 - n):
                forward(n, p, r, HALO, row_mask)
                if n:
                    backward(n, p, r, HALO, row_mask)
        each(first + n, last - n, strip)

    @pl.when(beside_x)
    def _():
        pl.semaphore_wait(late, 1)
        x_start(1)
        for a in range(3):
            c_copy(1, 1, a).start()

    each(2 * HALO, depth, finish, 1)

    @pl.loop(0, 2)
    def _(turn):
        high = lax.rem(odd + 1 + turn, 2)
        base = high * (depth + HALO)
        for side in range(2):
            @pl.when(high == side)
            def _():
                @pl.when(comes_from[0][side] if side else unless(comes_from[0][side], across))
                def _():
                    for j, a in x_parts(side):
                        x_copy(side, j, a).wait_recv()

                @pl.when(comes_from[0][side])
                def _():
                    for y_side in range(2):
                        there = comes_from[1][y_side]
                        if (side, y_side) == (0, 1):
                            there = unless(there, beside_x)

                            @pl.when(beside_x)
                            def _():
                                for a in range(3):
                                    e_copy(a).wait_recv()

                        @pl.when(there)
                        def _():
                            for a in range(3):
                                c_copy(side, y_side, a).wait_recv()

        there = jnp.where(high == 1, has_right, has_left)

        @pl.when(there)
        def _():
            @pl.loop(0, HALO)
            def _(j):
                fill(base + j, own0, rows, lambda i, m: (
                    xu[high, j, pl.ds(i, m), :], xm[high, j, pl.ds(i, m), :], xg[high, j, pl.ds(i, m), :]))
                other_way = both(beside_x, high == 0)

                @pl.when(other_way)
                def _():
                    fill(base + j, own0 + rows, HALO, lambda i, m: (
                        eu[j, pl.ds(0, HALO), :], em[j, pl.ds(0, HALO), :], eg[j, pl.ds(0, HALO), :]))

                for y_side in range(2):
                    @pl.when(unless(comes_from[1][y_side], other_way) if y_side else comes_from[1][y_side])
                    def _():
                        fill(base + j, R0 if y_side == 0 else own0 + rows, HALO, lambda i, m: (
                            cu[high, y_side, j], cm[high, y_side, j], cg[high, y_side, j]))

        @pl.when(jnp.logical_not(there))
        def _():
            @pl.loop(0, HALO)
            def _(j):
                blank(base + j, R0, ext)

        @pl.loop(0, HALO)
        def _(j):
            faces_x(high * (depth + HALO - 1) + j, R0, ext)

        def plane_mask(p):
            inside = jnp.logical_or(there, jnp.logical_and(p >= HALO, p < HALO + depth))
            scale = jnp.where(inside, 1.0, 0.0).astype(jnp.float32)
            return lambda s, m: M[pl.ds(s, m), :] * scale

        def start(p):
            faces(p, R0, ext)
            start_z(p, R0, ext, plane_mask(p))

        lo = 1 + high * (depth + 2)
        each(lo, lo + HALO, start)
        for n in range(3):
            def shell(p):
                forward(n, p, R0 + 1 + n, ext - 2 - 2 * n, plane_mask(p))
                if n:
                    backward(n, p, R0 + 1 + n, ext - 2 - 2 * n, plane_mask(p))
            begin = lo + n - 2 * n * high
            each(begin, begin + HALO, shell)
        begin = HALO + high * (depth - HALO)
        each(begin, begin + HALO, finish, 1)

    for side in range(2):
        @pl.when(sends_to[1][side])
        def _():
            for part in range(3):
                for a in range(3):
                    y_copy(side, part, a).wait_send()
        @pl.when(sends_to[0][side])
        def _():
            for j, a in x_parts(side):
                x_copy(side, j, a).wait_send()
        for y_side in range(2):
            @pl.when(both(comes_from[1][y_side], c_sent(side, y_side)))
            def _():
                for a in range(3):
                    c_copy(side, y_side, a).wait_send()

    @pl.when(across)
    def _():
        for a in range(3):
            e_copy(a).wait_send()


def put_out(a, b, a_out, b_out, sem):
    part = a.shape[0] // 4
    copies = [
        pltpu.make_async_copy(src.at[pl.ds(q * part, part)], dst.at[pl.ds(q * part, part)], sem.at[i, q])
        for i, (src, dst) in enumerate(((a, a_out), (b, b_out))) for q in range(4)
    ]
    for copy in copies:
        copy.start()
    for copy in copies:
        copy.wait()


def solution(mesh):
    nx, ny = mesh.shape["gx"], mesh.shape["gy"]

    def step(initial, material, goal_faces, conductivity):
        depth, rows, lanes = initial.shape
        planes, tall = depth + 2 * HALO, rows + 2 * HALO + 16
        f32, i32 = jnp.float32, jnp.int32
        by_rows = (depth, rows // HALO, HALO, lanes)
        halos = []
        for shape in ((2, HALO, rows, lanes), (2, depth, HALO, lanes), (2, 2, HALO, HALO, lanes),
                      (HALO, 2 * HALO, lanes)):
            halos += [pltpu.VMEM(shape, t) for t in (f32, i32, i32)]
        sem = pltpu.SemaphoreType.DMA
        whole = pl.BlockSpec(memory_space=pltpu.MemorySpace.HBM)
        inside = pl.BlockSpec(memory_space=pltpu.VMEM)

        def keep(v):
            return pltpu.with_memory_space_constraint(v, pltpu.MemorySpace.HBM)

        args = (conductivity, initial, material, goal_faces,
                initial.reshape(by_rows), material.reshape(by_rows), goal_faces.reshape(by_rows))
        ind, sens = pl.pallas_call(
            functools.partial(kernel, nx, ny),
            out_shape=[pltpu.VMEM(initial.shape, f32)] * 2,
            in_specs=[whole] * 7,
            out_specs=[inside, inside],
            scratch_shapes=[pltpu.VMEM((depth, rows, lanes), t) for t in (f32, i32, i32)]
            + halos
            + [pltpu.VMEM((planes, tall, lanes), f32) for _ in range(16)]
            + [pltpu.VMEM((tall, lanes), f32), pltpu.VMEM((3, tall, lanes), f32)]
            + [pltpu.SMEM(conductivity.shape, f32), sem((4,)), sem((2, HALO, 3)), sem((2, HALO, 3)),
               sem((2, 3, 3)), sem((2, 3, 3)), sem((2, 2, 3)), sem((2, 2, 3)), sem((3,)), sem((3,)),
               pltpu.SemaphoreType.REGULAR],
            compiler_params=pltpu.CompilerParams(
                collective_id=0, has_side_effects=True, vmem_limit_bytes=50 << 20),
            name="cells",
        )(*(keep(v) for v in args))
        return pl.pallas_call(
            put_out,
            out_shape=[jax.ShapeDtypeStruct(initial.shape, f32)] * 2,
            in_specs=[inside] * 2,
            out_specs=[pl.BlockSpec(memory_space=pl.ANY)] * 2,
            scratch_shapes=[sem((2, 4))],
            compiler_params=pltpu.CompilerParams(vmem_limit_bytes=4 << 20),
            name="put_out",
        )(ind, sens)

    placed = P("gx", "gy", None)
    return jax.shard_map(
        step,
        mesh=mesh,
        in_specs=(placed, placed, placed, P()),
        out_specs=(placed, placed),
        check_vma=False,
    )
```

```python
import functools

import jax
import jax.numpy as jnp
from jax import lax
from jax.experimental import pallas as pl
from jax.experimental.pallas import tpu as pltpu
from jax.sharding import PartitionSpec as P

MESH = pl.DeviceIdType.MESH
step_size = 0.075
HALO = 4
R0 = 8
CHUNK = 8
FINISH = 2


def kernel(
    nx, ny, cond_in,
    u_in, m_in, g_in, u_rows, m_rows, g_rows,
    ind_out, sens_out,
    u_all, m_all, g_all, u_edge, m_edge, g_edge, eu, em, eg,
    K, WX, WY, WZ, WB, C, G, V0, V1, V2, V3, Z3, Z2, Z1, S3, S2, M, T,
    cond, load_sem, x_send, x_recv, y_send, y_recv, c_send, c_recv, e_send, e_recv, late,
):
    depth, rows, lanes = u_in.shape
    V, Z, S = (V0, V1, V2, V3), (Z3, Z2, Z1), (S3, S2)
    groups = u_rows.shape[1]
    ext = rows + 2 * HALO
    own0 = R0 + HALO
    gx, gy = lax.axis_index("gx"), lax.axis_index("gy")
    has_left, has_right = gx > 0, gx < nx - 1
    has_down, has_up = gy > 0, gy < ny - 1
    left, right = (gx - 1, gy), (gx + 1, gy)
    down, up = (gx, gy - 1), (gx, gy + 1)
    odd = lax.rem(gx, 2)

    both, either = jnp.logical_and, jnp.logical_or
    is_first = both(gx == 0, gy == 0)
    beside_x, beside_y = both(gx == 1, gy == 0), both(gx == 0, gy == 1)
    across = both(gx == 1, gy == 1)
    beside = either(beside_x, beside_y)

    def unless(cond, but):
        return both(cond, jnp.logical_not(but))

    barrier = pltpu.get_barrier_semaphore()
    sides = ((has_left, left), (has_right, right), (has_down, down), (has_up, up))
    for there, who in sides:
        @pl.when(unless(there, is_first))
        def _():
            pl.semaphore_signal(barrier, inc=1, device_id=who, device_id_type=MESH)

    own_planes = pl.ds(HALO, depth)
    loads = [
        pltpu.make_async_copy(src, dst, load_sem.at[i])
        for i, (src, dst) in enumerate((
            (cond_in, cond), (m_in, m_all.at[own_planes]), (u_in, u_all.at[own_planes]), (g_in, g_all.at[own_planes])))
    ]
    for load in loads:
        load.start()

    ins, in_rows = (u_in, m_in, g_in), (u_rows, m_rows, g_rows)
    alls, edges_of = (u_all, m_all, g_all), (u_edge, m_edge, g_edge)

    def remote(src, dst, send, recv, who):
        return pltpu.make_async_remote_copy(
            src_ref=src, dst_ref=dst, send_sem=send, recv_sem=recv,
            device_id=who, device_id_type=MESH,
        )

    def y_copies(side):
        who = (gx, gy + 1 - 2 * side)
        return [
            remote(in_rows[a].at[:, (1 - side) * (groups - 1)], edges_of[a].at[side, own_planes],
                   y_send.at[side, a], y_recv.at[side, a], who)
            for a in range(3)
        ]

    def x_copies(side):
        who = (gx + 1 - 2 * side, gy)
        first, place = (1 - side) * (depth - HALO), side * (depth + HALO)
        return [
            remote(ins[a].at[pl.ds(first + skip, n)], alls[a].at[pl.ds(place + skip, n)],
                   x_send.at[side, i], x_recv.at[side, i], who)
            for i, (a, skip, n) in enumerate(((1, 0, HALO), (0, 0, HALO), (2, 0, HALO - 1)))
        ]

    def x_last(side):
        who = (gx + 1 - 2 * side, gy)
        return remote(g_in.at[depth - 1], g_all.at[HALO - 1], x_send.at[0, 3], x_recv.at[0, 3], who)

    def c_copies(side, y_side):
        who = (gx + 1 - 2 * side, gy)
        first, place = HALO + (1 - side) * (depth - HALO), side * (depth + HALO)
        return [
            remote(edges_of[a].at[y_side, pl.ds(first, HALO)], edges_of[a].at[y_side, pl.ds(place, HALO)],
                   c_send.at[side, y_side, a], c_recv.at[side, y_side, a], who)
            for a in range(3)
        ]

    def e_copies():
        return [
            remote(alls[a].at[pl.ds(0, HALO), pl.ds(0, 2 * HALO)], (eu, em, eg)[a],
                   e_send.at[a], e_recv.at[a], down)
            for a in range(3)
        ]

    def pick(side, low, high):
        return either(both(side == 0, low), both(side == 1, high))

    def x_to(side):
        return pick(side, has_right, has_left)

    def x_from(side):
        return pick(side, has_left, has_right)

    def y_to(side):
        return pick(side, has_up, has_down)

    def y_from(side):
        return pick(side, has_down, has_up)

    def c_sent(side, y_side):
        way = unless(x_to(side), both(is_first, both(side == 0, y_side == 1)))
        return both(y_from(y_side), way)

    def start_all(copies):
        for copy in copies:
            copy.start()

    def x_start(side):
        start_all(x_copies(side))

        @pl.when(side == 0)
        def _():
            x_last(side).start()

    def x_arrive(side):
        for copy in x_copies(side):
            copy.wait_recv()

        @pl.when(side == 0)
        def _():
            x_last(side).wait_recv()

    def turned(v):
        return pltpu.roll(v, lanes - 1, 1), pltpu.roll(v, 1, 1)

    def lane_is(which, n):
        return lax.broadcasted_iota(jnp.int32, (n, lanes), 1) == which

    def ends_off(a, b):
        n = a.shape[0]
        return jnp.where(lane_is(lanes - 1, n), 0.0, a), jnp.where(lane_is(0, n), 0.0, b)

    def chunks(r, n):
        while n > 0:
            yield r, min(n, CHUNK)
            r, n = r + CHUNK, n - CHUNK

    def fill(p, r, n, there, read):
        for i in range(0, n, CHUNK):
            m = min(CHUNK, n - i)
            uv, mv, gv = read(i, m)
            at = pl.ds(r + i, m)
            k = jnp.full(mv.shape, table[0], jnp.float32)
            for w in range(1, len(table)):
                k = jnp.where(mv == w, table[w], k)
            K[p, at, :] = jnp.where(there, k, 0.0)
            V[0][p, at, :] = jnp.where(there, uv, 0.0)
            G[p, at, :] = jnp.where(there, gv.astype(jnp.float32), 0.0)

    def fill_own(p, there):
        fill(p, own0, rows, there, lambda i, m: tuple(ref[p, pl.ds(i, m), :] for ref in alls))

    def fill_edges(p, there):
        for side, r in ((0, R0), (1, own0 + rows)):
            fill(p, r, HALO, both(there, y_from(side)), lambda i, m: tuple(ref[side, p] for ref in edges_of))

    def faces_x(p, r, n):
        for s, m in chunks(r, n):
            at = pl.ds(s, m)
            WX[p, at, :] = K[p, at, :] + K[p + 1, at, :]

    def faces(p, r, n, scale):
        for s, m in chunks(r, n):
            at, lo, hi = pl.ds(s, m), pl.ds(s - 1, m), pl.ds(s + 1, m)
            k = K[p, at, :]
            a, b = ends_off(*turned(k))
            h = K[p, hi, :]
            k2 = k + k
            WY[p, at, :] = k + h
            WZ[p, at, :] = jnp.where(lane_is(lanes - 1, m), 0.0, k + a)
            WB[p, at, :] = jnp.where(lane_is(0, m), 0.0, k + b)
            wx, wx_low = WX[p, at, :], WX[p - 1, at, :]
            C[p, at, :] = ((wx + wx_low) + (k2 + (K[p, lo, :] + h))) + (k2 + (a + b))
            Z[0][p, at, :] = (G[p, at, :] * wx - G[p - 1, at, :] * wx_low) * (M[at, :] * scale)

    def spread(src, p, s, m):
        at, lo, hi = pl.ds(s, m), pl.ds(s - 1, m), pl.ds(s + 1, m)
        v = src[p, at, :]
        a, b = turned(v)
        d = (
            (WX[p, at, :] * src[p + 1, at, :] + WX[p - 1, at, :] * src[p - 1, at, :])
            + (WY[p, at, :] * src[p, hi, :] + WY[p, lo, :] * src[p, lo, :])
            + (WZ[p, at, :] * a + WB[p, at, :] * b)
            - C[p, at, :] * v
        )
        return v, a, b, d

    def forward(n, p, r, k, scale):
        for s, m in chunks(r, k):
            at = pl.ds(s, m)
            V[n + 1][p, at, :] = spread(V[n], p, s, m)[3] * (M[at, :] * scale)

    def backward(n, p, r, k, scale):
        for s, m in chunks(r, k):
            v, a, b, d = spread(Z[n - 1], p, s, m)
            at = pl.ds(s, m)
            Z[n][p, at, :] = v + d * (M[at, :] * scale)
            a, b = ends_off(a, b)
            S[n - 1][p, at, :] = v + (a + b)

    def finish(p, slot):
        for i, z in enumerate((Z1, S2, S3)):
            for s, m in chunks(own0 - 1, rows + 2):
                at = pl.ds(s, m)
                T[slot, i, at, :] = z[p - 1, at, :] + z[p, at, :] + z[p + 1, at, :]
        for s, m in chunks(own0, rows):
            at, lo, hi = pl.ds(s, m), pl.ds(s - 1, m), pl.ds(s + 1, m)
            e1, e2, e3 = V2[p, at, :], V3[p, at, :], spread(V3, p, s, m)[3]
            z1, _, _, d = spread(Z1, p, s, m)
            r1 = e1 + e2
            r2 = r1 + (e2 + e3)
            sums = [T[slot, i, lo, :] + T[slot, i, at, :] + T[slot, i, hi, :] for i in range(3)]
            a, b = ends_off(*turned(sums[0]))
            q1 = sums[0] + (a + b)
            third = 1.0 / 27.0
            total = (e1 * (q1 * third - z1) + r1 * (sums[1] * third - Z2[p, at, :])
                     + r2 * (sums[2] * third - Z[0][p, at, :]))
            out = pl.ds(s - own0, m)
            ind_out[p - HALO, out, :] = total * (-1.0 / (step_size * step_size))
            sens_out[p - HALO, out, :] = (z1 + d) * (1.0 / step_size)

    def each(lo, count, body, unroll=2):
        @pl.loop(0, count // unroll)
        def _(i):
            for j in range(unroll):
                body(lo + i * unroll + j, j)

    pl.semaphore_wait(barrier, sum(there.astype(jnp.int32) for there, _ in sides) - beside.astype(jnp.int32))

    @pl.when(is_first)
    def _():
        for who in (right, up):
            pl.semaphore_signal(late, inc=1, device_id=who, device_id_type=MESH)

    @pl.loop(0, 2)
    def _(side):
        @pl.when(unless(y_to(side), both(beside_y, side == 1)))
        def _():
            start_all(y_copies(side))

        @pl.when(unless(x_to(side), both(beside_x, side == 1)))
        def _():
            x_start(side)

    for load in loads:
        load.wait()
    table = [cond[i] * (0.5 * step_size) for i in range(cond.shape[0])]
    row = lax.broadcasted_iota(jnp.int32, (ext, lanes), 0)
    M[pl.ds(R0, ext), :] = jnp.where(
        both(either(row >= HALO, has_down), either(row < HALO + rows, has_up)), 1.0, 0.0).astype(jnp.float32)
    edge_tiles = (R0, own0 + rows - HALO)

    @pl.loop(0, 3)
    def _(turn):
        own = turn == 0
        high = jnp.where(turn == 1, 1 - odd, odd)
        there = either(own, x_from(high))

        def begin(low_own, low, step):
            return jnp.where(own, low_own, low + step * high)

        def plane_scale(p):
            inside = either(there, both(p >= HALO, p < HALO + depth))
            return jnp.where(inside, 1.0, 0.0).astype(jnp.float32)

        @pl.when(both(there, turn > 0))
        def _():
            @pl.when(unless(turn > 0, both(across, high == 0)))
            def _():
                x_arrive(high)

            other_way = both(beside_x, high == 0)

            @pl.when(other_way)
            def _():
                for copy in e_copies():
                    copy.wait_recv()
                for got, ref in zip((eu, em, eg), edges_of):
                    for j in range(HALO):
                        ref[1, j] = got[j, pl.ds(0, HALO), :]

            @pl.loop(0, 2)
            def _(y_side):
                @pl.when(unless(y_from(y_side), both(other_way, y_side == 1)))
                def _():
                    for copy in c_copies(high, y_side):
                        copy.wait_recv()

        fill_lo = begin(HALO, 0, depth + HALO)
        fill_n = jnp.where(own, depth, HALO)

        @pl.loop(0, fill_n)
        def _(j):
            fill_own(fill_lo + j, there)

        def edges_in():
            @pl.loop(0, fill_n)
            def _(j):
                fill_edges(fill_lo + j, there)

        x_lo, x_n = begin(HALO, 0, depth + HALO - 1), jnp.where(own, depth - 1, HALO)
        lo, step = begin(HALO + 1, 1, depth + 2), jnp.where(own, 1, 1 - 2 * high)

        def count(n):
            return jnp.where(own, depth - 2 - 2 * n, HALO)

        pl.when(turn > 0)(edges_in)

        @pl.loop(0, x_n)
        def _(j):
            faces_x(x_lo + j, R0, ext)

        each(lo, count(0), lambda p, j: faces(p, R0, ext, plane_scale(p)))
        each(lo, count(0), lambda p, j: forward(0, p, R0 + 1, ext - 2, plane_scale(p)))

        for n in (1, 2):
            def both_ways(p, j):
                forward(n, p, R0 + 1, ext - 2, plane_scale(p))
                backward(n, p, R0 + 1, ext - 2, plane_scale(p))
            each(lo + n * step, count(n), both_ways)

        @pl.when(own)
        def _():
            @pl.when(beside_y)
            def _():
                pl.semaphore_wait(late, 1)
                start_all(y_copies(1))

            @pl.when(across)
            def _():
                x_arrive(0)
                start_all(e_copies())

            @pl.when(beside_x)
            def _():
                pl.semaphore_wait(late, 1)
                x_start(1)

            @pl.loop(0, 2)
            def _(y_side):
                @pl.when(y_from(y_side))
                def _():
                    for copy in y_copies(y_side):
                        copy.wait_recv()

                    @pl.loop(0, 2)
                    def _(side):
                        @pl.when(c_sent(side, y_side))
                        def _():
                            start_all(c_copies(side, y_side))

            edges_in()

            @pl.loop(0, x_n)
            def _(j):
                for r in edge_tiles:
                    faces_x(x_lo + j, r, 2 * HALO)

            def edge_faces(p, j):
                for r in edge_tiles:
                    faces(p, r, 2 * HALO, 1.0)
            each(lo, count(0), edge_faces)

            def edge_forward(p, j):
                for r in edge_tiles:
                    forward(0, p, r, 2 * HALO, 1.0)
            each(lo, count(0), edge_forward)

            for n in (1, 2):
                def edge_both(p, j):
                    for r in edge_tiles:
                        forward(n, p, r, 2 * HALO, 1.0)
                        backward(n, p, r, 2 * HALO, 1.0)
                each(lo + n, count(n), edge_both)

        each(begin(2 * HALO, HALO, depth - HALO), jnp.where(own, depth - 2 * HALO, HALO), finish, FINISH)

    @pl.loop(0, 2)
    def _(side):
        @pl.when(y_to(side))
        def _():
            for copy in y_copies(side):
                copy.wait_send()

        @pl.when(x_to(side))
        def _():
            for copy in x_copies(side):
                copy.wait_send()

            @pl.when(side == 0)
            def _():
                x_last(side).wait_send()

        @pl.loop(0, 2)
        def _(y_side):
            @pl.when(c_sent(side, y_side))
            def _():
                for copy in c_copies(side, y_side):
                    copy.wait_send()

    @pl.when(across)
    def _():
        for copy in e_copies():
            copy.wait_send()


def put_out(a, b, a_out, b_out, sem):
    part = a.shape[0] // 4
    copies = [
        pltpu.make_async_copy(src.at[pl.ds(q * part, part)], dst.at[pl.ds(q * part, part)], sem.at[i, q])
        for i, (src, dst) in enumerate(((a, a_out), (b, b_out))) for q in range(4)
    ]
    for copy in copies:
        copy.start()
    for copy in copies:
        copy.wait()


def solution(mesh):
    nx, ny = mesh.shape["gx"], mesh.shape["gy"]

    def step(initial, material, goal_faces, conductivity):
        depth, rows, lanes = initial.shape
        planes, tall = depth + 2 * HALO, rows + 2 * HALO + 16
        f32, i32 = jnp.float32, jnp.int32
        by_rows = (depth, rows // HALO, HALO, lanes)
        halos = []
        for shape in ((planes, rows, lanes), (2, planes, HALO, lanes), (HALO, 2 * HALO, lanes)):
            halos += [pltpu.VMEM(shape, t) for t in (f32, i32, i32)]
        sem = pltpu.SemaphoreType.DMA
        whole = pl.BlockSpec(memory_space=pltpu.MemorySpace.HBM)
        inside = pl.BlockSpec(memory_space=pltpu.VMEM)

        def keep(v):
            return pltpu.with_memory_space_constraint(v, pltpu.MemorySpace.HBM)

        args = (conductivity, initial, material, goal_faces,
                initial.reshape(by_rows), material.reshape(by_rows), goal_faces.reshape(by_rows))
        ind, sens = pl.pallas_call(
            functools.partial(kernel, nx, ny),
            out_shape=[pltpu.VMEM(initial.shape, f32)] * 2,
            in_specs=[whole] * 7,
            out_specs=[inside, inside],
            scratch_shapes=halos
            + [pltpu.VMEM((planes, tall, lanes), f32) for _ in range(16)]
            + [pltpu.VMEM((tall, lanes), f32), pltpu.VMEM((FINISH, 3, tall, lanes), f32)]
            + [pltpu.SMEM(conductivity.shape, f32), sem((4,)), sem((2, 4)), sem((2, 4)),
               sem((2, 3)), sem((2, 3)), sem((2, 2, 3)), sem((2, 2, 3)), sem((3,)), sem((3,)),
               pltpu.SemaphoreType.REGULAR],
            compiler_params=pltpu.CompilerParams(
                collective_id=0, has_side_effects=True, vmem_limit_bytes=50 << 20),
            name="cells",
        )(*(keep(v) for v in args))
        return pl.pallas_call(
            put_out,
            out_shape=[jax.ShapeDtypeStruct(initial.shape, f32)] * 2,
            in_specs=[inside] * 2,
            out_specs=[pl.BlockSpec(memory_space=pl.ANY)] * 2,
            scratch_shapes=[sem((2, 4))],
            compiler_params=pltpu.CompilerParams(vmem_limit_bytes=4 << 20),
            name="put_out",
        )(ind, sens)

    placed = P("gx", "gy", None)
    return jax.shard_map(
        step,
        mesh=mesh,
        in_specs=(placed, placed, placed, P()),
        out_specs=(placed, placed),
        check_vma=False,
    )
```

```python
import functools

import jax
import jax.numpy as jnp
from jax import lax
from jax.experimental import pallas as pl
from jax.experimental.pallas import tpu as pltpu
from jax.sharding import PartitionSpec as P

MESH = pl.DeviceIdType.MESH
step_size = 0.075
HALO = 4
R0 = 8
CHUNK = 8
FINISH = 2


def kernel(
    nx, ny, cond_in,
    u_in, m_in, g_in, u_rows, m_rows, g_rows,
    ind_out, sens_out,
    u_all, m_all, g_all, u_edge, m_edge, g_edge, eu, em, eg,
    K, WX, WY, WZ, WB, C, G, V0, V1, V2, V3, Z3, Z2, Z1, S3, S2, M, T,
    cond, load_sem, x_send, x_recv, y_send, y_recv, c_send, c_recv, e_send, e_recv, late,
):
    depth, rows, lanes = u_in.shape
    V, Z, S = (V0, V1, V2, V3), (Z3, Z2, Z1), (S3, S2)
    groups = u_rows.shape[1]
    ext = rows + 2 * HALO
    own0 = R0 + HALO
    gx, gy = lax.axis_index("gx"), lax.axis_index("gy")
    has_left, has_right = gx > 0, gx < nx - 1
    has_down, has_up = gy > 0, gy < ny - 1
    left, right = (gx - 1, gy), (gx + 1, gy)
    down, up = (gx, gy - 1), (gx, gy + 1)
    odd = lax.rem(gx, 2)

    both, either = jnp.logical_and, jnp.logical_or
    is_first = both(gx == 0, gy == 0)
    beside_x, beside_y = both(gx == 1, gy == 0), both(gx == 0, gy == 1)
    across = both(gx == 1, gy == 1)
    beside = either(beside_x, beside_y)

    def unless(cond, but):
        return both(cond, jnp.logical_not(but))

    barrier = pltpu.get_barrier_semaphore()
    sides = ((has_left, left), (has_right, right), (has_down, down), (has_up, up))
    for there, who in sides:
        @pl.when(unless(there, is_first))
        def _():
            pl.semaphore_signal(barrier, inc=1, device_id=who, device_id_type=MESH)

    own_planes = pl.ds(HALO, depth)
    loads = [
        pltpu.make_async_copy(src, dst, load_sem.at[i])
        for i, (src, dst) in enumerate((
            (cond_in, cond), (m_in, m_all.at[own_planes]), (u_in, u_all.at[own_planes]), (g_in, g_all.at[own_planes])))
    ]
    for load in loads:
        load.start()

    ins, in_rows = (u_in, m_in, g_in), (u_rows, m_rows, g_rows)
    alls, edges_of = (u_all, m_all, g_all), (u_edge, m_edge, g_edge)

    def remote(src, dst, send, recv, who):
        return pltpu.make_async_remote_copy(
            src_ref=src, dst_ref=dst, send_sem=send, recv_sem=recv,
            device_id=who, device_id_type=MESH,
        )

    def y_copies(side):
        who = (gx, gy + 1 - 2 * side)
        return [
            remote(in_rows[a].at[:, (1 - side) * (groups - 1)], edges_of[a].at[side, own_planes],
                   y_send.at[side, a], y_recv.at[side, a], who)
            for a in range(3)
        ]

    def x_copies(side):
        who = (gx + 1 - 2 * side, gy)
        first, place = (1 - side) * (depth - HALO), side * (depth + HALO)
        return [
            remote(ins[a].at[pl.ds(first + skip, n)], alls[a].at[pl.ds(place + skip, n)],
                   x_send.at[side, i], x_recv.at[side, i], who)
            for i, (a, skip, n) in enumerate(((1, 0, HALO), (0, 0, HALO), (2, 0, HALO - 1)))
        ]

    def x_last(side):
        who = (gx + 1 - 2 * side, gy)
        return remote(g_in.at[depth - 1], g_all.at[HALO - 1], x_send.at[0, 3], x_recv.at[0, 3], who)

    def c_copies(side, y_side):
        who = (gx + 1 - 2 * side, gy)
        first, place = HALO + (1 - side) * (depth - HALO), side * (depth + HALO)
        return [
            remote(edges_of[a].at[y_side, pl.ds(first, HALO)], edges_of[a].at[y_side, pl.ds(place, HALO)],
                   c_send.at[side, y_side, a], c_recv.at[side, y_side, a], who)
            for a in range(3)
        ]

    def e_copies():
        return [
            remote(alls[a].at[pl.ds(0, HALO), pl.ds(0, 2 * HALO)], (eu, em, eg)[a],
                   e_send.at[a], e_recv.at[a], down)
            for a in range(3)
        ]

    def pick(side, low, high):
        return either(both(side == 0, low), both(side == 1, high))

    def x_to(side):
        return pick(side, has_right, has_left)

    def x_from(side):
        return pick(side, has_left, has_right)

    def y_to(side):
        return pick(side, has_up, has_down)

    def y_from(side):
        return pick(side, has_down, has_up)

    def c_sent(side, y_side):
        way = unless(x_to(side), both(is_first, both(side == 0, y_side == 1)))
        return both(y_from(y_side), way)

    def start_all(copies):
        for copy in copies:
            copy.start()

    def x_start(side):
        start_all(x_copies(side))

        @pl.when(side == 0)
        def _():
            x_last(side).start()

    def x_arrive(side):
        for copy in x_copies(side):
            copy.wait_recv()

        @pl.when(side == 0)
        def _():
            x_last(side).wait_recv()

    def turned(v):
        return pltpu.roll(v, lanes - 1, 1), pltpu.roll(v, 1, 1)

    def lane_is(which, n):
        return lax.broadcasted_iota(jnp.int32, (n, lanes), 1) == which

    def ends_off(a, b):
        n = a.shape[0]
        return jnp.where(lane_is(lanes - 1, n), 0.0, a), jnp.where(lane_is(0, n), 0.0, b)

    def chunks(r, n):
        while n > 0:
            yield r, min(n, CHUNK)
            r, n = r + CHUNK, n - CHUNK

    def fill(p, r, n, there, read):
        for i in range(0, n, CHUNK):
            m = min(CHUNK, n - i)
            uv, mv, gv = read(i, m)
            at = pl.ds(r + i, m)
            k = jnp.full(mv.shape, table[0], jnp.float32)
            for w in range(1, len(table)):
                k = jnp.where(mv == w, table[w], k)
            K[p, at, :] = jnp.where(there, k, 0.0)
            V[0][p, at, :] = jnp.where(there, uv, 0.0)
            G[p, at, :] = jnp.where(there, gv.astype(jnp.float32), 0.0)

    def fill_own(p, there):
        fill(p, own0, rows, there, lambda i, m: tuple(ref[p, pl.ds(i, m), :] for ref in alls))

    def fill_edges(p, there):
        for side, r in ((0, R0), (1, own0 + rows)):
            fill(p, r, HALO, both(there, y_from(side)), lambda i, m: tuple(ref[side, p] for ref in edges_of))

    def faces(p, r, n, scale):
        for s, m in chunks(r, n):
            at, lo, hi = pl.ds(s, m), pl.ds(s - 1, m), pl.ds(s + 1, m)
            k, behind = K[p, at, :], K[p - 1, at, :]
            a, b = ends_off(*turned(k))
            h = K[p, hi, :]
            k2 = k + k
            WY[p, at, :] = k + h
            WZ[p, at, :] = jnp.where(lane_is(lanes - 1, m), 0.0, k + a)
            WB[p, at, :] = jnp.where(lane_is(0, m), 0.0, k + b)
            wx, wx_low = k + K[p + 1, at, :], behind + k
            WX[p, at, :], WX[p - 1, at, :] = wx, wx_low
            C[p, at, :] = ((wx + wx_low) + (k2 + (K[p, lo, :] + h))) + (k2 + (a + b))
            Z[0][p, at, :] = (G[p, at, :] * wx - G[p - 1, at, :] * wx_low) * (M[at, :] * scale)

    def spread(src, p, s, m):
        at, lo, hi = pl.ds(s, m), pl.ds(s - 1, m), pl.ds(s + 1, m)
        v = src[p, at, :]
        a, b = turned(v)
        d = (
            (WX[p, at, :] * src[p + 1, at, :] + WX[p - 1, at, :] * src[p - 1, at, :])
            + (WY[p, at, :] * src[p, hi, :] + WY[p, lo, :] * src[p, lo, :])
            + (WZ[p, at, :] * a + WB[p, at, :] * b)
            - C[p, at, :] * v
        )
        return v, a, b, d

    def forward(n, p, r, k, scale):
        for s, m in chunks(r, k):
            at = pl.ds(s, m)
            V[n + 1][p, at, :] = spread(V[n], p, s, m)[3] * (M[at, :] * scale)

    def backward(n, p, r, k, scale):
        for s, m in chunks(r, k):
            v, a, b, d = spread(Z[n - 1], p, s, m)
            at = pl.ds(s, m)
            Z[n][p, at, :] = v + d * (M[at, :] * scale)
            a, b = ends_off(a, b)
            S[n - 1][p, at, :] = v + (a + b)

    def finish(p, slot):
        for i, z in enumerate((Z1, S2, S3)):
            for s, m in chunks(own0 - 1, rows + 2):
                at = pl.ds(s, m)
                T[slot, i, at, :] = z[p - 1, at, :] + z[p, at, :] + z[p + 1, at, :]
        for s, m in chunks(own0, rows):
            at, lo, hi = pl.ds(s, m), pl.ds(s - 1, m), pl.ds(s + 1, m)
            e1, e2, e3 = V2[p, at, :], V3[p, at, :], spread(V3, p, s, m)[3]
            z1, _, _, d = spread(Z1, p, s, m)
            r1 = e1 + e2
            r2 = r1 + (e2 + e3)
            sums = [T[slot, i, lo, :] + T[slot, i, at, :] + T[slot, i, hi, :] for i in range(3)]
            a, b = ends_off(*turned(sums[0]))
            q1 = sums[0] + (a + b)
            third = 1.0 / 27.0
            total = (e1 * (q1 * third - z1) + r1 * (sums[1] * third - Z2[p, at, :])
                     + r2 * (sums[2] * third - Z[0][p, at, :]))
            out = pl.ds(s - own0, m)
            ind_out[p - HALO, out, :] = total * (-1.0 / (step_size * step_size))
            sens_out[p - HALO, out, :] = (z1 + d) * (1.0 / step_size)

    def each(lo, count, body, unroll=2):
        @pl.loop(0, count // unroll)
        def _(i):
            for j in range(unroll):
                body(lo + i * unroll + j, j)

    pl.semaphore_wait(barrier, sum(there.astype(jnp.int32) for there, _ in sides) - beside.astype(jnp.int32))

    @pl.when(is_first)
    def _():
        for who in (right, up):
            pl.semaphore_signal(late, inc=1, device_id=who, device_id_type=MESH)

    @pl.loop(0, 2)
    def _(side):
        @pl.when(unless(y_to(side), both(beside_y, side == 1)))
        def _():
            start_all(y_copies(side))

        @pl.when(unless(x_to(side), both(beside_x, side == 1)))
        def _():
            x_start(side)

    for load in loads:
        load.wait()
    table = [cond[i] * (0.5 * step_size) for i in range(cond.shape[0])]
    row = lax.broadcasted_iota(jnp.int32, (ext, lanes), 0)
    M[pl.ds(R0, ext), :] = jnp.where(
        both(either(row >= HALO, has_down), either(row < HALO + rows, has_up)), 1.0, 0.0).astype(jnp.float32)

    near = 1 - odd

    def corners_in(high):
        other_way = both(beside_x, high == 0)

        @pl.when(other_way)
        def _():
            for copy in e_copies():
                copy.wait_recv()
            for got, ref in zip((eu, em, eg), edges_of):
                for j in range(HALO):
                    ref[1, j] = got[j, pl.ds(0, HALO), :]

        @pl.loop(0, 2)
        def _(y_side):
            @pl.when(unless(y_from(y_side), both(other_way, y_side == 1)))
            def _():
                for copy in c_copies(high, y_side):
                    copy.wait_recv()

    def pair(p, j, tiles, scales):
        if j == 0:
            for q, scale in enumerate(scales):
                for r, n in tiles:
                    faces(p + q, r, n, scale)
            for q, scale in enumerate(scales):
                for r, n in tiles:
                    forward(0, p + q, max(r, R0 + 1), min(n, ext - 2), scale)

    @pl.loop(0, 3 + beside_x.astype(jnp.int32))
    def _(turn):
        own, last = turn == 0, turn >= 2
        high = jnp.where(unless(last, both(beside_x, turn == 2)), odd, near)
        idle = both(beside_x, turn == 1)
        there = either(own, x_from(high))

        def plane_scale(p):
            inside = either(there, both(p >= HALO, p < HALO + depth))
            return jnp.where(inside, 1.0, 0.0).astype(jnp.float32)

        @pl.when(both(there, unless(turn > 0, idle)))
        def _():
            x_arrive(high)

            @pl.when(both(across, turn == 1))
            def _():
                start_all(e_copies())

            @pl.when(last)
            def _():
                corners_in(high)

        def span(own):
            fill_lo = jnp.where(own, HALO, (depth + HALO) * high)
            lo, step = jnp.where(own, HALO + 1, 1 + (depth + 2) * high), jnp.where(own, 1, 1 - 2 * high)
            return fill_lo, jnp.where(own, depth, HALO), lo, step

        def count(own, n):
            return jnp.where(own, depth - 2 - 2 * n, HALO)

        fill_lo, fill_n, lo, step = span(own)

        @pl.loop(0, jnp.where(idle, 0, fill_n))
        def _(j):
            fill_own(fill_lo + j, there)

        @pl.when(last)
        def _():
            each(fill_lo, HALO, lambda p, j: fill_edges(p, there), HALO)

        each(lo, jnp.where(idle, 0, count(own, 0)), lambda p, j: pair(p, j, ((R0, ext),), (plane_scale(p), plane_scale(p + 1))))
        for n in (1, 2):
            def both_ways(p, j):
                forward(n, p, R0 + 1, ext - 2, plane_scale(p))
                backward(n, p, R0 + 1, ext - 2, plane_scale(p))
            each(lo + n * step, jnp.where(idle, 0, count(own, n)), both_ways)

        @pl.when(turn == 1)
        def _():
            @pl.when(beside_y)
            def _():
                pl.semaphore_wait(late, 1)
                start_all(y_copies(1))

            @pl.loop(0, 2)
            def _(y_side):
                @pl.when(y_from(y_side))
                def _():
                    for copy in y_copies(y_side):
                        copy.wait_recv()

                    @pl.loop(0, 2)
                    def _(side):
                        @pl.when(unless(c_sent(side, y_side), both(beside_x, side == 1)))
                        def _():
                            start_all(c_copies(side, y_side))

            tiles = ((R0, 2 * HALO), (own0 + rows - HALO, 2 * HALO))

            @pl.loop(0, jnp.where(idle, 1, 2))
            def _(part):
                mine = part == 0
                pl.when(part == 1)(lambda: corners_in(near))
                fill_lo, fill_n, lo, step = span(mine)
                each(fill_lo, fill_n, lambda p, j: fill_edges(p, True), HALO)
                each(lo, count(mine, 0), lambda p, j: pair(p, j, tiles, (1.0, 1.0)))
                for n in (1, 2):
                    def edge_both(p, j):
                        for r, m in tiles:
                            forward(n, p, r, m, 1.0)
                            backward(n, p, r, m, 1.0)
                    each(lo + n * step, count(mine, n), edge_both)

            @pl.when(beside_x)
            def _():
                pl.semaphore_wait(late, 1)
                x_start(1)
                start_all(c_copies(1, 1))

        done_lo = jnp.where(last, HALO + high * (depth - HALO), jnp.where(idle, 2 * HALO, HALO + high * HALO))
        done_n = jnp.where(last, HALO, jnp.where(idle, depth - 2 * HALO, depth - HALO))
        each(done_lo, jnp.where(own, 0, done_n), finish, FINISH)

    @pl.loop(0, 2)
    def _(side):
        @pl.when(y_to(side))
        def _():
            for copy in y_copies(side):
                copy.wait_send()

        @pl.when(x_to(side))
        def _():
            for copy in x_copies(side):
                copy.wait_send()

            @pl.when(side == 0)
            def _():
                x_last(side).wait_send()

        @pl.loop(0, 2)
        def _(y_side):
            @pl.when(c_sent(side, y_side))
            def _():
                for copy in c_copies(side, y_side):
                    copy.wait_send()

    @pl.when(across)
    def _():
        for copy in e_copies():
            copy.wait_send()


def put_out(a, b, a_out, b_out, sem):
    part = a.shape[0] // 4
    copies = [
        pltpu.make_async_copy(src.at[pl.ds(q * part, part)], dst.at[pl.ds(q * part, part)], sem.at[i, q])
        for i, (src, dst) in enumerate(((a, a_out), (b, b_out))) for q in range(4)
    ]
    for copy in copies:
        copy.start()
    for copy in copies:
        copy.wait()


def solution(mesh):
    nx, ny = mesh.shape["gx"], mesh.shape["gy"]

    def step(initial, material, goal_faces, conductivity):
        depth, rows, lanes = initial.shape
        planes, tall = depth + 2 * HALO, rows + 2 * HALO + 16
        f32, i32 = jnp.float32, jnp.int32
        by_rows = (depth, rows // HALO, HALO, lanes)
        halos = []
        for shape in ((planes, rows, lanes), (2, planes, HALO, lanes), (HALO, 2 * HALO, lanes)):
            halos += [pltpu.VMEM(shape, t) for t in (f32, i32, i32)]
        sem = pltpu.SemaphoreType.DMA
        whole = pl.BlockSpec(memory_space=pltpu.MemorySpace.HBM)
        inside = pl.BlockSpec(memory_space=pltpu.VMEM)

        def keep(v):
            return pltpu.with_memory_space_constraint(v, pltpu.MemorySpace.HBM)

        args = (conductivity, initial, material, goal_faces,
                initial.reshape(by_rows), material.reshape(by_rows), goal_faces.reshape(by_rows))
        ind, sens = pl.pallas_call(
            functools.partial(kernel, nx, ny),
            out_shape=[pltpu.VMEM(initial.shape, f32)] * 2,
            in_specs=[whole] * 7,
            out_specs=[inside, inside],
            scratch_shapes=halos
            + [pltpu.VMEM((planes, tall, lanes), f32) for _ in range(16)]
            + [pltpu.VMEM((tall, lanes), f32), pltpu.VMEM((FINISH, 3, tall, lanes), f32)]
            + [pltpu.SMEM(conductivity.shape, f32), sem((4,)), sem((2, 4)), sem((2, 4)),
               sem((2, 3)), sem((2, 3)), sem((2, 2, 3)), sem((2, 2, 3)), sem((3,)), sem((3,)),
               pltpu.SemaphoreType.REGULAR],
            compiler_params=pltpu.CompilerParams(
                collective_id=0, has_side_effects=True, vmem_limit_bytes=50 << 20),
            name="cells",
        )(*(keep(v) for v in args))
        return pl.pallas_call(
            put_out,
            out_shape=[jax.ShapeDtypeStruct(initial.shape, f32)] * 2,
            in_specs=[inside] * 2,
            out_specs=[pl.BlockSpec(memory_space=pl.ANY)] * 2,
            scratch_shapes=[sem((2, 4))],
            compiler_params=pltpu.CompilerParams(vmem_limit_bytes=4 << 20),
            name="put_out",
        )(ind, sens)

    placed = P("gx", "gy", None)
    return jax.shard_map(
        step,
        mesh=mesh,
        in_specs=(placed, placed, placed, P()),
        out_specs=(placed, placed),
        check_vma=False,
    )
```

```python
import functools

import jax
import jax.numpy as jnp
from jax import lax
from jax.experimental import pallas as pl
from jax.experimental.pallas import tpu as pltpu
from jax.sharding import PartitionSpec as P

MESH = pl.DeviceIdType.MESH
step_size = 0.075
HALO = 4
R0 = 8
CHUNK = 8
FINISH = 2
LANES = 128


def turned(v):
    return pltpu.roll(v, LANES - 1, 1), pltpu.roll(v, 1, 1)


def lane_is(which, n):
    return lax.broadcasted_iota(jnp.int32, (n, LANES), 1) == which


def ends_off(a, b):
    n = a.shape[0]
    return jnp.where(lane_is(LANES - 1, n), 0.0, a), jnp.where(lane_is(0, n), 0.0, b)


def chunks(r, n):
    while n > 0:
        yield r, min(n, CHUNK)
        r, n = r + CHUNK, n - CHUNK


def each(lo, count, body, unroll=2):
    @pl.loop(0, count // unroll)
    def _(i):
        for j in range(unroll):
            body(lo + i * unroll + j, j)


def spread_with(weights, src, p, s, m):
    WX, WY, WZ, WB, C = weights
    at, lo, hi = pl.ds(s, m), pl.ds(s - 1, m), pl.ds(s + 1, m)
    v = src[p, at, :]
    a, b = turned(v)
    d = (
        (WX[p, at, :] * src[p + 1, at, :] + WX[p - 1, at, :] * src[p - 1, at, :])
        + (WY[p, at, :] * src[p, hi, :] + WY[p, lo, :] * src[p, lo, :])
        + (WZ[p, at, :] * a + WB[p, at, :] * b)
        - C[p, at, :] * v
    )
    return v, a, b, d


def finish(weights, fields, T, outs, p, slot, tiles):
    V2, V3, Z3, Z2, Z1, S3, S2 = fields
    own0 = R0 + HALO
    for r, n in tiles:
        for i, z in enumerate((Z1, S2, S3)):
            for s, m in chunks(r - 1, n + 2):
                at = pl.ds(s, m)
                T[slot, i, at, :] = z[p - 1, at, :] + z[p, at, :] + z[p + 1, at, :]
    for r, n in tiles:
        for s, m in chunks(r, n):
            at, lo, hi = pl.ds(s, m), pl.ds(s - 1, m), pl.ds(s + 1, m)
            e1, e2, e3 = V2[p, at, :], V3[p, at, :], spread_with(weights, V3, p, s, m)[3]
            z1, _, _, d = spread_with(weights, Z1, p, s, m)
            r1 = e1 + e2
            r2 = r1 + (e2 + e3)
            sums = [T[slot, i, lo, :] + T[slot, i, at, :] + T[slot, i, hi, :] for i in range(3)]
            a, b = ends_off(*turned(sums[0]))
            q1 = sums[0] + (a + b)
            third = 1.0 / 27.0
            total = (e1 * (q1 * third - z1) + r1 * (sums[1] * third - Z2[p, at, :])
                     + r2 * (sums[2] * third - Z3[p, at, :])) * (-1.0 / (step_size * step_size))
            out = pl.ds(s - own0, m)
            outs[0][p - HALO, out, :] = total
            outs[1][p - HALO, out, :] = (z1 + d) * (1.0 / step_size)


def kernel(
    nx, ny, cond_in,
    u_in, m_in, g_in, u_rows, m_rows, g_rows,
    ind_out, sens_out, WX, WY, WZ, WB, C, V2, V3, Z3, Z2, Z1, S3, S2,
    u_all, m_all, g_all, u_edge, m_edge, g_edge, eu, em, eg,
    K, G, V0, V1, M, T,
    cond, load_sem, x_send, x_recv, y_send, y_recv, c_send, c_recv, e_send, e_recv, late,
):
    depth, rows, lanes = u_in.shape
    V, Z, S = (V0, V1, V2, V3), (Z3, Z2, Z1), (S3, S2)
    groups = u_rows.shape[1]
    ext = rows + 2 * HALO
    own0 = R0 + HALO
    gx, gy = lax.axis_index("gx"), lax.axis_index("gy")
    has_left, has_right = gx > 0, gx < nx - 1
    has_down, has_up = gy > 0, gy < ny - 1
    left, right = (gx - 1, gy), (gx + 1, gy)
    down, up = (gx, gy - 1), (gx, gy + 1)
    odd = lax.rem(gx, 2)

    both, either = jnp.logical_and, jnp.logical_or
    is_first = both(gx == 0, gy == 0)
    beside_x, beside_y = both(gx == 1, gy == 0), both(gx == 0, gy == 1)
    across = both(gx == 1, gy == 1)
    beside = either(beside_x, beside_y)

    def unless(cond, but):
        return both(cond, jnp.logical_not(but))

    barrier = pltpu.get_barrier_semaphore()
    sides = ((has_left, left), (has_right, right), (has_down, down), (has_up, up))
    for there, who in sides:
        @pl.when(unless(there, is_first))
        def _():
            pl.semaphore_signal(barrier, inc=1, device_id=who, device_id_type=MESH)

    own_planes = pl.ds(HALO, depth)
    loads = [
        pltpu.make_async_copy(src, dst, load_sem.at[i])
        for i, (src, dst) in enumerate((
            (cond_in, cond), (m_in, m_all.at[own_planes]), (u_in, u_all.at[own_planes]), (g_in, g_all.at[own_planes])))
    ]
    for load in loads:
        load.start()

    ins, in_rows = (u_in, m_in, g_in), (u_rows, m_rows, g_rows)
    alls, edges_of = (u_all, m_all, g_all), (u_edge, m_edge, g_edge)

    def remote(src, dst, send, recv, who):
        return pltpu.make_async_remote_copy(
            src_ref=src, dst_ref=dst, send_sem=send, recv_sem=recv,
            device_id=who, device_id_type=MESH,
        )

    def y_copies(side):
        who = (gx, gy + 1 - 2 * side)
        return [
            remote(in_rows[a].at[:, (1 - side) * (groups - 1)], edges_of[a].at[side, own_planes],
                   y_send.at[side, a], y_recv.at[side, a], who)
            for a in range(3)
        ]

    def x_copies(side):
        who = (gx + 1 - 2 * side, gy)
        first, place = (1 - side) * (depth - HALO), side * (depth + HALO)
        return [
            remote(ins[a].at[pl.ds(first + skip, n)], alls[a].at[pl.ds(place + skip, n)],
                   x_send.at[side, i], x_recv.at[side, i], who)
            for i, (a, skip, n) in enumerate(((1, 0, HALO), (0, 0, HALO), (2, 0, HALO - 1)))
        ]

    def x_last(side):
        who = (gx + 1 - 2 * side, gy)
        return remote(g_in.at[depth - 1], g_all.at[HALO - 1], x_send.at[0, 3], x_recv.at[0, 3], who)

    def c_copies(side, y_side):
        who = (gx + 1 - 2 * side, gy)
        first, place = HALO + (1 - side) * (depth - HALO), side * (depth + HALO)
        return [
            remote(edges_of[a].at[y_side, pl.ds(first, HALO)], edges_of[a].at[y_side, pl.ds(place, HALO)],
                   c_send.at[side, y_side, a], c_recv.at[side, y_side, a], who)
            for a in range(3)
        ]

    def e_copies():
        return [
            remote(alls[a].at[pl.ds(0, HALO), pl.ds(0, 2 * HALO)], (eu, em, eg)[a],
                   e_send.at[a], e_recv.at[a], down)
            for a in range(3)
        ]

    def pick(side, low, high):
        return either(both(side == 0, low), both(side == 1, high))

    def x_to(side):
        return pick(side, has_right, has_left)

    def x_from(side):
        return pick(side, has_left, has_right)

    def y_to(side):
        return pick(side, has_up, has_down)

    def y_from(side):
        return pick(side, has_down, has_up)

    def c_sent(side, y_side):
        way = unless(x_to(side), both(is_first, both(side == 0, y_side == 1)))
        return both(y_from(y_side), way)

    def start_all(copies):
        for copy in copies:
            copy.start()

    def x_start(side):
        start_all(x_copies(side))

        @pl.when(side == 0)
        def _():
            x_last(side).start()

    def x_arrive(side):
        for copy in x_copies(side):
            copy.wait_recv()

        @pl.when(side == 0)
        def _():
            x_last(side).wait_recv()

    def fill(p, r, n, there, read):
        for i in range(0, n, CHUNK):
            m = min(CHUNK, n - i)
            uv, mv, gv = read(i, m)
            at = pl.ds(r + i, m)
            k = jnp.full(mv.shape, table[0], jnp.float32)
            for w in range(1, len(table)):
                k = jnp.where(mv == w, table[w], k)
            K[p, at, :] = jnp.where(there, k, 0.0)
            V[0][p, at, :] = jnp.where(there, uv, 0.0)
            G[p, at, :] = jnp.where(there, gv.astype(jnp.float32), 0.0)

    def fill_own(p, there):
        fill(p, own0, rows, there, lambda i, m: tuple(ref[p, pl.ds(i, m), :] for ref in alls))

    def fill_edges(p, there):
        for side, r in ((0, R0), (1, own0 + rows)):
            fill(p, r, HALO, both(there, y_from(side)), lambda i, m: tuple(ref[side, p] for ref in edges_of))

    def kept(s, m, scale):
        if own0 <= s and s + m <= own0 + rows:
            return scale
        return M[pl.ds(s, m), :] * scale

    def faces(p, r, n, scale):
        for s, m in chunks(r, n):
            at, lo, hi = pl.ds(s, m), pl.ds(s - 1, m), pl.ds(s + 1, m)
            k, behind = K[p, at, :], K[p - 1, at, :]
            a, b = ends_off(*turned(k))
            h = K[p, hi, :]
            k2 = k + k
            WY[p, at, :] = k + h
            WZ[p, at, :] = jnp.where(lane_is(lanes - 1, m), 0.0, k + a)
            WB[p, at, :] = jnp.where(lane_is(0, m), 0.0, k + b)
            wx, wx_low = k + K[p + 1, at, :], behind + k
            WX[p, at, :], WX[p - 1, at, :] = wx, wx_low
            C[p, at, :] = ((wx + wx_low) + (k2 + (K[p, lo, :] + h))) + (k2 + (a + b))
            Z[0][p, at, :] = (G[p, at, :] * wx - G[p - 1, at, :] * wx_low) * kept(s, m, scale)

    weights = (WX, WY, WZ, WB, C)
    fields = (V2, V3, Z3, Z2, Z1, S3, S2)

    def spread(src, p, s, m):
        return spread_with(weights, src, p, s, m)

    def forward(n, p, r, k, scale):
        for s, m in chunks(r, k):
            at = pl.ds(s, m)
            V[n + 1][p, at, :] = spread(V[n], p, s, m)[3] * kept(s, m, scale)

    def backward(n, p, r, k, scale):
        for s, m in chunks(r, k):
            v, a, b, d = spread(Z[n - 1], p, s, m)
            at = pl.ds(s, m)
            Z[n][p, at, :] = v + d * kept(s, m, scale)
            a, b = ends_off(a, b)
            S[n - 1][p, at, :] = v + (a + b)

    pl.semaphore_wait(barrier, sum(there.astype(jnp.int32) for there, _ in sides) - beside.astype(jnp.int32))

    @pl.when(is_first)
    def _():
        for who in (right, up):
            pl.semaphore_signal(late, inc=1, device_id=who, device_id_type=MESH)

    @pl.loop(0, 2)
    def _(side):
        @pl.when(unless(y_to(side), both(beside_y, side == 1)))
        def _():
            start_all(y_copies(side))

        @pl.when(unless(x_to(side), both(beside_x, side == 1)))
        def _():
            x_start(side)

    for load in loads:
        load.wait()
    table = [cond[i] * (0.5 * step_size) for i in range(cond.shape[0])]
    row = lax.broadcasted_iota(jnp.int32, (ext, lanes), 0)
    M[pl.ds(R0, ext), :] = jnp.where(
        both(either(row >= HALO, has_down), either(row < HALO + rows, has_up)), 1.0, 0.0).astype(jnp.float32)

    near = 1 - odd

    def corners_in(high):
        other_way = both(beside_x, high == 0)

        @pl.when(other_way)
        def _():
            for copy in e_copies():
                copy.wait_recv()
            for got, ref in zip((eu, em, eg), edges_of):
                for j in range(HALO):
                    ref[1, j] = got[j, pl.ds(0, HALO), :]

        @pl.loop(0, 2)
        def _(y_side):
            @pl.when(unless(y_from(y_side), both(other_way, y_side == 1)))
            def _():
                for copy in c_copies(high, y_side):
                    copy.wait_recv()

    def pair(p, j, tiles, scales):
        if j == 0:
            for q, scale in enumerate(scales):
                for r, n in tiles:
                    faces(p + q, r, n, scale)
            for q, scale in enumerate(scales):
                for r, n in tiles:
                    forward(0, p + q, max(r, R0 + 1), min(n, ext - 2), scale)

    @pl.loop(0, 3 + beside_x.astype(jnp.int32))
    def _(turn):
        own, last = turn == 0, turn >= 2
        high = jnp.where(unless(last, both(beside_x, turn == 2)), odd, near)
        idle = both(beside_x, turn == 1)
        there = either(own, x_from(high))

        def plane_scale(p):
            inside = either(there, both(p >= HALO, p < HALO + depth))
            return jnp.where(inside, 1.0, 0.0).astype(jnp.float32)

        @pl.when(both(there, unless(turn > 0, idle)))
        def _():
            x_arrive(high)

            @pl.when(both(across, turn == 1))
            def _():
                start_all(e_copies())

            @pl.when(last)
            def _():
                corners_in(high)

        def span(own):
            fill_lo = jnp.where(own, HALO, (depth + HALO) * high)
            lo, step = jnp.where(own, HALO + 1, 1 + (depth + 2) * high), jnp.where(own, 1, 1 - 2 * high)
            return fill_lo, jnp.where(own, depth, HALO), lo, step

        def count(own, n):
            return jnp.where(own, depth - 2 - 2 * n, HALO)

        fill_lo, fill_n, lo, step = span(own)

        @pl.loop(0, jnp.where(idle, 0, fill_n))
        def _(j):
            fill_own(fill_lo + j, there)

        @pl.when(last)
        def _():
            each(fill_lo, HALO, lambda p, j: fill_edges(p, there), HALO)

        each(lo, jnp.where(idle, 0, count(own, 0)), lambda p, j: pair(p, j, ((R0, ext),), (plane_scale(p), plane_scale(p + 1))))
        for n in (1, 2):
            def both_ways(p, j):
                forward(n, p, R0 + 1, ext - 2, plane_scale(p))
                backward(n, p, R0 + 1, ext - 2, plane_scale(p))
            each(lo + n * step, jnp.where(idle, 0, count(own, n)), both_ways)

        @pl.when(turn == 1)
        def _():
            @pl.when(beside_y)
            def _():
                pl.semaphore_wait(late, 1)
                start_all(y_copies(1))

            @pl.loop(0, 2)
            def _(y_side):
                @pl.when(y_from(y_side))
                def _():
                    for copy in y_copies(y_side):
                        copy.wait_recv()

                    @pl.loop(0, 2)
                    def _(side):
                        @pl.when(unless(c_sent(side, y_side), both(beside_x, side == 1)))
                        def _():
                            start_all(c_copies(side, y_side))

            tiles = ((R0, 2 * HALO), (own0 + rows - HALO, 2 * HALO))

            @pl.loop(0, jnp.where(idle, 1, 2))
            def _(part):
                mine = part == 0
                pl.when(part == 1)(lambda: corners_in(near))
                fill_lo, fill_n, lo, step = span(mine)
                each(fill_lo, fill_n, lambda p, j: fill_edges(p, True), HALO)
                each(lo, count(mine, 0), lambda p, j: pair(p, j, tiles, (1.0, 1.0)))
                for n in (1, 2):
                    def edge_both(p, j):
                        for r, m in tiles:
                            forward(n, p, r, m, 1.0)
                            backward(n, p, r, m, 1.0)
                    each(lo + n * step, count(mine, n), edge_both)

            @pl.when(beside_x)
            def _():
                pl.semaphore_wait(late, 1)
                x_start(1)
                start_all(c_copies(1, 1))

        late_turn = both(beside_x, turn == 2)
        done_lo = jnp.where(last, HALO + high * (depth - HALO), jnp.where(idle, 2 * HALO, HALO + high * HALO))
        done_n = jnp.where(turn == 1, jnp.where(idle, depth - 2 * HALO, depth - HALO), jnp.where(late_turn, HALO, 0))
        each(done_lo, done_n, lambda p, j: finish(
            weights, fields, T, (ind_out, sens_out), p, j, ((own0, rows),)), FINISH)

    @pl.loop(0, 2)
    def _(side):
        @pl.when(y_to(side))
        def _():
            for copy in y_copies(side):
                copy.wait_send()

        @pl.when(x_to(side))
        def _():
            for copy in x_copies(side):
                copy.wait_send()

            @pl.when(side == 0)
            def _():
                x_last(side).wait_send()

        @pl.loop(0, 2)
        def _(y_side):
            @pl.when(c_sent(side, y_side))
            def _():
                for copy in c_copies(side, y_side):
                    copy.wait_send()

    @pl.when(across)
    def _():
        for copy in e_copies():
            copy.wait_send()


def put_out(*refs):
    done, refs = refs[:2], refs[2:]
    weights, fields, outs, last, T, sem = refs[:5], refs[5:12], refs[12:14], refs[14:16], refs[16], refs[17]
    depth, rows, _ = done[0].shape
    odd = lax.rem(lax.axis_index("gx"), 2)
    first, part = HALO * (1 - odd), (depth - HALO) // 3
    copies = [
        pltpu.make_async_copy(done[i].at[at], outs[i].at[at], sem.at[i, q])
        for q in range(3) for i in range(2) for at in (pl.ds(first + q * part, part),)
    ]
    for copy in copies:
        copy.start()
    begin = HALO + odd * (depth - HALO)
    own0 = R0 + HALO
    each(begin, HALO, lambda p, j: finish(weights, fields, T, last, p, j, ((own0, rows),)), FINISH)
    at = pl.ds(odd * (depth - HALO), HALO)
    rest = [pltpu.make_async_copy(last[i].at[at], outs[i].at[at], sem.at[i, 3]) for i in range(2)]
    for copy in rest:
        copy.start()
    for copy in copies + rest:
        copy.wait()


def solution(mesh):
    nx, ny = mesh.shape["gx"], mesh.shape["gy"]

    def step(initial, material, goal_faces, conductivity):
        depth, rows, lanes = initial.shape
        planes, tall = depth + 2 * HALO, rows + 2 * HALO + 16
        f32, i32 = jnp.float32, jnp.int32
        by_rows = (depth, rows // HALO, HALO, lanes)
        halos = []
        for shape in ((planes, rows, lanes), (2, planes, HALO, lanes), (HALO, 2 * HALO, lanes)):
            halos += [pltpu.VMEM(shape, t) for t in (f32, i32, i32)]
        sem = pltpu.SemaphoreType.DMA
        whole = pl.BlockSpec(memory_space=pltpu.MemorySpace.HBM)
        inside = pl.BlockSpec(memory_space=pltpu.VMEM)

        def keep(v):
            return pltpu.with_memory_space_constraint(v, pltpu.MemorySpace.HBM)

        args = (conductivity, initial, material, goal_faces,
                initial.reshape(by_rows), material.reshape(by_rows), goal_faces.reshape(by_rows))
        field = pltpu.VMEM((planes, tall, lanes), f32)
        block = pltpu.VMEM(initial.shape, f32)
        made = pl.pallas_call(
            functools.partial(kernel, nx, ny),
            out_shape=[block] * 2 + [field] * 12,
            in_specs=[whole] * 7,
            out_specs=[inside] * 14,
            scratch_shapes=halos
            + [field] * 4
            + [pltpu.VMEM((tall, lanes), f32), pltpu.VMEM((FINISH, 3, tall, lanes), f32)]
            + [pltpu.SMEM(conductivity.shape, f32), sem((4,)), sem((2, 4)), sem((2, 4)),
               sem((2, 3)), sem((2, 3)), sem((2, 2, 3)), sem((2, 2, 3)), sem((3,)), sem((3,)),
               pltpu.SemaphoreType.REGULAR],
            compiler_params=pltpu.CompilerParams(
                collective_id=0, has_side_effects=True, vmem_limit_bytes=30 << 20),
            name="cells",
        )(*(keep(v) for v in args))
        return pl.pallas_call(
            put_out,
            out_shape=[jax.ShapeDtypeStruct(initial.shape, f32)] * 2,
            in_specs=[inside] * 14,
            out_specs=[pl.BlockSpec(memory_space=pl.ANY)] * 2,
            scratch_shapes=[block] * 2 + [pltpu.VMEM((FINISH, 3, tall, lanes), f32), sem((2, 4))],
            compiler_params=pltpu.CompilerParams(vmem_limit_bytes=8 << 20),
            name="put_out",
        )(*made)

    placed = P("gx", "gy", None)
    return jax.shard_map(
        step,
        mesh=mesh,
        in_specs=(placed, placed, placed, P()),
        out_specs=(placed, placed),
        check_vma=False,
    )
```

```python
import functools

import jax
import jax.numpy as jnp
from jax import lax
from jax.experimental import pallas as pl
from jax.experimental.pallas import tpu as pltpu
from jax.sharding import PartitionSpec as P

MESH = pl.DeviceIdType.MESH
step_size = 0.075
HALO = 4
R0 = 8
CHUNK = 8
FINISH = 2
LANES = 128


def turned(v):
    return pltpu.roll(v, LANES - 1, 1), pltpu.roll(v, 1, 1)


def lane_is(which, n):
    return lax.broadcasted_iota(jnp.int32, (n, LANES), 1) == which


def ends_off(a, b):
    n = a.shape[0]
    return jnp.where(lane_is(LANES - 1, n), 0.0, a), jnp.where(lane_is(0, n), 0.0, b)


def chunks(r, n):
    while n > 0:
        yield r, min(n, CHUNK)
        r, n = r + CHUNK, n - CHUNK


def each(lo, count, body, unroll=2):
    @pl.loop(0, count // unroll)
    def _(i):
        for j in range(unroll):
            body(lo + i * unroll + j, j)


def spread_with(weights, src, p, s, m):
    WX, WY, WZ, WB, C = weights
    at, lo, hi = pl.ds(s, m), pl.ds(s - 1, m), pl.ds(s + 1, m)
    v = src[p, at, :]
    a, b = turned(v)
    d = (
        (WX[p, at, :] * src[p + 1, at, :] + WX[p - 1, at, :] * src[p - 1, at, :])
        + (WY[p, at, :] * src[p, hi, :] + WY[p, lo, :] * src[p, lo, :])
        + (WZ[p, at, :] * a + WB[p, at, :] * b)
        - C[p, at, :] * v
    )
    return v, a, b, d


def finish(weights, fields, T, outs, p, slot, tiles):
    V2, V3, Z3, Z2, Z1, S3, S2 = fields
    own0 = R0 + HALO
    for r, n in tiles:
        for i, z in enumerate((Z1, S2, S3)):
            for s, m in chunks(r - 1, n + 2):
                at = pl.ds(s, m)
                T[slot, i, at, :] = z[p - 1, at, :] + z[p, at, :] + z[p + 1, at, :]
    for r, n in tiles:
        for s, m in chunks(r, n):
            at, lo, hi = pl.ds(s, m), pl.ds(s - 1, m), pl.ds(s + 1, m)
            e1, e2, e3 = V2[p, at, :], V3[p, at, :], spread_with(weights, V3, p, s, m)[3]
            z1, _, _, d = spread_with(weights, Z1, p, s, m)
            r1 = e1 + e2
            r2 = r1 + (e2 + e3)
            sums = [T[slot, i, lo, :] + T[slot, i, at, :] + T[slot, i, hi, :] for i in range(3)]
            a, b = ends_off(*turned(sums[0]))
            q1 = sums[0] + (a + b)
            third = 1.0 / 27.0
            total = (e1 * (q1 * third - z1) + r1 * (sums[1] * third - Z2[p, at, :])
                     + r2 * (sums[2] * third - Z3[p, at, :])) * (-1.0 / (step_size * step_size))
            out = pl.ds(s - own0, m)
            outs[0][p - HALO, out, :] = total
            outs[1][p - HALO, out, :] = (z1 + d) * (1.0 / step_size)


def kernel(
    nx, ny, cond_in,
    u_in, m_in, g_in, u_rows, m_rows, g_rows,
    ind_out, sens_out, WX, WY, WZ, WB, C, V2, V3, Z3, Z2, Z1, S3, S2,
    u_all, m_all, g_all, u_edge, m_edge, g_edge, eu, em, eg,
    K, G, V0, V1, M, T,
    cond, load_sem, x_send, x_recv, y_send, y_recv, c_send, c_recv, e_send, e_recv, late,
):
    depth, rows, lanes = u_in.shape
    V, Z, S = (V0, V1, V2, V3), (Z3, Z2, Z1), (S3, S2)
    groups = u_rows.shape[1]
    ext = rows + 2 * HALO
    own0 = R0 + HALO
    gx, gy = lax.axis_index("gx"), lax.axis_index("gy")
    has_left, has_right = gx > 0, gx < nx - 1
    has_down, has_up = gy > 0, gy < ny - 1
    left, right = (gx - 1, gy), (gx + 1, gy)
    down, up = (gx, gy - 1), (gx, gy + 1)
    odd = lax.rem(gx, 2)

    both, either = jnp.logical_and, jnp.logical_or
    is_first = both(gx == 0, gy == 0)
    beside_x, beside_y = both(gx == 1, gy == 0), both(gx == 0, gy == 1)
    across = both(gx == 1, gy == 1)
    beside = either(beside_x, beside_y)

    def unless(cond, but):
        return both(cond, jnp.logical_not(but))

    barrier = pltpu.get_barrier_semaphore()
    sides = ((has_left, left), (has_right, right), (has_down, down), (has_up, up))
    for there, who in sides:
        @pl.when(unless(there, is_first))
        def _():
            pl.semaphore_signal(barrier, inc=1, device_id=who, device_id_type=MESH)

    own_planes = pl.ds(HALO, depth)
    loads = [
        pltpu.make_async_copy(src, dst, load_sem.at[i])
        for i, (src, dst) in enumerate((
            (cond_in, cond), (m_in, m_all.at[own_planes]), (u_in, u_all.at[own_planes]), (g_in, g_all.at[own_planes])))
    ]
    for load in loads:
        load.start()

    ins, in_rows = (u_in, m_in, g_in), (u_rows, m_rows, g_rows)
    alls, edges_of = (u_all, m_all, g_all), (u_edge, m_edge, g_edge)

    def remote(src, dst, send, recv, who):
        return pltpu.make_async_remote_copy(
            src_ref=src, dst_ref=dst, send_sem=send, recv_sem=recv,
            device_id=who, device_id_type=MESH,
        )

    def y_copies(side):
        who = (gx, gy + 1 - 2 * side)
        return [
            remote(in_rows[a].at[:, (1 - side) * (groups - 1)], edges_of[a].at[side, own_planes],
                   y_send.at[side, a], y_recv.at[side, a], who)
            for a in range(3)
        ]

    def x_copies(side):
        who = (gx + 1 - 2 * side, gy)
        first, place = (1 - side) * (depth - HALO), side * (depth + HALO)
        return [
            remote(ins[a].at[pl.ds(first + skip, n)], alls[a].at[pl.ds(place + skip, n)],
                   x_send.at[side, i], x_recv.at[side, i], who)
            for i, (a, skip, n) in enumerate(((1, 0, HALO), (0, 0, HALO), (2, 0, HALO - 1)))
        ]

    def x_last(side):
        who = (gx + 1 - 2 * side, gy)
        return remote(g_in.at[depth - 1], g_all.at[HALO - 1], x_send.at[0, 3], x_recv.at[0, 3], who)

    def c_copies(side, y_side):
        who = (gx + 1 - 2 * side, gy)
        first, place = HALO + (1 - side) * (depth - HALO), side * (depth + HALO)
        return [
            remote(edges_of[a].at[y_side, pl.ds(first, HALO)], edges_of[a].at[y_side, pl.ds(place, HALO)],
                   c_send.at[side, y_side, a], c_recv.at[side, y_side, a], who)
            for a in range(3)
        ]

    def e_copies():
        return [
            remote(alls[a].at[pl.ds(0, HALO), pl.ds(0, 2 * HALO)], (eu, em, eg)[a],
                   e_send.at[a], e_recv.at[a], down)
            for a in range(3)
        ]

    def pick(side, low, high):
        return either(both(side == 0, low), both(side == 1, high))

    def x_to(side):
        return pick(side, has_right, has_left)

    def x_from(side):
        return pick(side, has_left, has_right)

    def y_to(side):
        return pick(side, has_up, has_down)

    def y_from(side):
        return pick(side, has_down, has_up)

    def c_sent(side, y_side):
        way = unless(x_to(side), both(is_first, both(side == 0, y_side == 1)))
        return both(y_from(y_side), way)

    def start_all(copies):
        for copy in copies:
            copy.start()

    def x_start(side):
        start_all(x_copies(side))

        @pl.when(side == 0)
        def _():
            x_last(side).start()

    def x_arrive(side):
        for copy in x_copies(side):
            copy.wait_recv()

        @pl.when(side == 0)
        def _():
            x_last(side).wait_recv()

    def fill(p, r, n, there, read):
        for i in range(0, n, CHUNK):
            m = min(CHUNK, n - i)
            uv, mv, gv = read(i, m)
            at = pl.ds(r + i, m)
            k = jnp.full(mv.shape, table[0], jnp.float32)
            for w in range(1, len(table)):
                k = jnp.where(mv == w, table[w], k)
            K[p, at, :] = jnp.where(there, k, 0.0)
            V[0][p, at, :] = jnp.where(there, uv, 0.0)
            G[p, at, :] = jnp.where(there, gv.astype(jnp.float32), 0.0)

    def fill_own(p, there):
        fill(p, own0, rows, there, lambda i, m: tuple(ref[p, pl.ds(i, m), :] for ref in alls))

    def fill_edges(p, there):
        for side, r in ((0, R0), (1, own0 + rows)):
            fill(p, r, HALO, both(there, y_from(side)), lambda i, m: tuple(ref[side, p] for ref in edges_of))

    def kept(s, m, scale):
        if own0 <= s and s + m <= own0 + rows:
            return scale
        return M[pl.ds(s, m), :] * scale

    def faces(p, r, n, scale):
        for s, m in chunks(r, n):
            at, lo, hi = pl.ds(s, m), pl.ds(s - 1, m), pl.ds(s + 1, m)
            k, behind = K[p, at, :], K[p - 1, at, :]
            a, b = ends_off(*turned(k))
            h = K[p, hi, :]
            k2 = k + k
            WY[p, at, :] = k + h
            WZ[p, at, :] = jnp.where(lane_is(lanes - 1, m), 0.0, k + a)
            WB[p, at, :] = jnp.where(lane_is(0, m), 0.0, k + b)
            wx, wx_low = k + K[p + 1, at, :], behind + k
            WX[p, at, :], WX[p - 1, at, :] = wx, wx_low
            C[p, at, :] = ((wx + wx_low) + (k2 + (K[p, lo, :] + h))) + (k2 + (a + b))
            Z[0][p, at, :] = (G[p, at, :] * wx - G[p - 1, at, :] * wx_low) * kept(s, m, scale)

    weights = (WX, WY, WZ, WB, C)
    fields = (V2, V3, Z3, Z2, Z1, S3, S2)

    def spread(src, p, s, m):
        return spread_with(weights, src, p, s, m)

    def forward(n, p, r, k, scale):
        for s, m in chunks(r, k):
            at = pl.ds(s, m)
            V[n + 1][p, at, :] = spread(V[n], p, s, m)[3] * kept(s, m, scale)

    def backward(n, p, r, k, scale):
        for s, m in chunks(r, k):
            v, a, b, d = spread(Z[n - 1], p, s, m)
            at = pl.ds(s, m)
            Z[n][p, at, :] = v + d * kept(s, m, scale)
            a, b = ends_off(a, b)
            S[n - 1][p, at, :] = v + (a + b)

    pl.semaphore_wait(barrier, sum(there.astype(jnp.int32) for there, _ in sides) - beside.astype(jnp.int32))

    @pl.when(is_first)
    def _():
        for who in (right, up):
            pl.semaphore_signal(late, inc=1, device_id=who, device_id_type=MESH)

    @pl.loop(0, 2)
    def _(side):
        @pl.when(unless(y_to(side), both(beside_y, side == 1)))
        def _():
            start_all(y_copies(side))

    @pl.loop(0, 2)
    def _(side):
        @pl.when(unless(x_to(side), both(beside_x, side == 1)))
        def _():
            x_start(side)

    for load in loads:
        load.wait()
    table = [cond[i] * (0.5 * step_size) for i in range(cond.shape[0])]
    row = lax.broadcasted_iota(jnp.int32, (ext, lanes), 0)
    M[pl.ds(R0, ext), :] = jnp.where(
        both(either(row >= HALO, has_down), either(row < HALO + rows, has_up)), 1.0, 0.0).astype(jnp.float32)

    near = 1 - odd

    def corners_in(high):
        other_way = both(beside_x, high == 0)

        @pl.when(other_way)
        def _():
            for copy in e_copies():
                copy.wait_recv()
            for got, ref in zip((eu, em, eg), edges_of):
                for j in range(HALO):
                    ref[1, j] = got[j, pl.ds(0, HALO), :]

        @pl.loop(0, 2)
        def _(y_side):
            @pl.when(unless(y_from(y_side), both(other_way, y_side == 1)))
            def _():
                for copy in c_copies(high, y_side):
                    copy.wait_recv()

    def pair(p, j, tiles, scales):
        if j == 0:
            for q, scale in enumerate(scales):
                for r, n in tiles:
                    faces(p + q, r, n, scale)
            for q, scale in enumerate(scales):
                for r, n in tiles:
                    forward(0, p + q, max(r, R0 + 1), min(n, ext - 2), scale)

    @pl.loop(0, 3 + beside_x.astype(jnp.int32))
    def _(turn):
        own, last = turn == 0, turn >= 2
        high = jnp.where(unless(last, both(beside_x, turn == 2)), odd, near)
        idle = both(beside_x, turn == 1)
        there = either(own, x_from(high))

        def plane_scale(p):
            inside = either(there, both(p >= HALO, p < HALO + depth))
            return jnp.where(inside, 1.0, 0.0).astype(jnp.float32)

        @pl.when(both(there, unless(turn > 0, idle)))
        def _():
            x_arrive(high)

            @pl.when(both(across, turn == 1))
            def _():
                start_all(e_copies())

            @pl.when(last)
            def _():
                corners_in(high)

        def span(own):
            fill_lo = jnp.where(own, HALO, (depth + HALO) * high)
            lo, step = jnp.where(own, HALO + 1, 1 + (depth + 2) * high), jnp.where(own, 1, 1 - 2 * high)
            return fill_lo, jnp.where(own, depth, HALO), lo, step

        def count(own, n):
            return jnp.where(own, depth - 2 - 2 * n, HALO)

        fill_lo, fill_n, lo, step = span(own)

        @pl.loop(0, jnp.where(idle, 0, fill_n))
        def _(j):
            fill_own(fill_lo + j, there)

        @pl.when(last)
        def _():
            each(fill_lo, HALO, lambda p, j: fill_edges(p, there), HALO)

        each(lo, jnp.where(idle, 0, count(own, 0)), lambda p, j: pair(p, j, ((R0, ext),), (plane_scale(p), plane_scale(p + 1))))
        for n in (1, 2):
            def both_ways(p, j):
                forward(n, p, R0 + 1, ext - 2, plane_scale(p))
                backward(n, p, R0 + 1, ext - 2, plane_scale(p))
            each(lo + n * step, jnp.where(idle, 0, count(own, n)), both_ways)

        @pl.when(turn == 1)
        def _():
            @pl.when(beside_y)
            def _():
                pl.semaphore_wait(late, 1)
                start_all(y_copies(1))

            @pl.loop(0, 2)
            def _(y_side):
                @pl.when(y_from(y_side))
                def _():
                    for copy in y_copies(y_side):
                        copy.wait_recv()

                    @pl.loop(0, 2)
                    def _(side):
                        @pl.when(unless(c_sent(side, y_side), both(beside_x, side == 1)))
                        def _():
                            start_all(c_copies(side, y_side))

            tiles = ((R0, 2 * HALO), (own0 + rows - HALO, 2 * HALO))

            @pl.loop(0, jnp.where(idle, 1, 2))
            def _(part):
                mine = part == 0
                pl.when(part == 1)(lambda: corners_in(near))
                fill_lo, fill_n, lo, step = span(mine)
                each(fill_lo, fill_n, lambda p, j: fill_edges(p, True), HALO)
                each(lo, count(mine, 0), lambda p, j: pair(p, j, tiles, (1.0, 1.0)))
                for n in (1, 2):
                    def edge_both(p, j):
                        for r, m in tiles:
                            forward(n, p, r, m, 1.0)
                            backward(n, p, r, m, 1.0)
                    each(lo + n * step, count(mine, n), edge_both)

            @pl.when(beside_x)
            def _():
                pl.semaphore_wait(late, 1)
                x_start(1)
                start_all(c_copies(1, 1))

        late_turn = both(beside_x, turn == 2)
        done_lo = jnp.where(last, HALO + high * (depth - HALO), jnp.where(idle, 2 * HALO, HALO + high * HALO))
        done_n = jnp.where(turn == 1, jnp.where(idle, depth - 2 * HALO, depth - HALO), jnp.where(late_turn, HALO, 0))
        each(done_lo, done_n, lambda p, j: finish(
            weights, fields, T, (ind_out, sens_out), p, j, ((own0, rows),)), FINISH)

    @pl.loop(0, 2)
    def _(side):
        @pl.when(y_to(side))
        def _():
            for copy in y_copies(side):
                copy.wait_send()

        @pl.when(x_to(side))
        def _():
            for copy in x_copies(side):
                copy.wait_send()

            @pl.when(side == 0)
            def _():
                x_last(side).wait_send()

        @pl.loop(0, 2)
        def _(y_side):
            @pl.when(c_sent(side, y_side))
            def _():
                for copy in c_copies(side, y_side):
                    copy.wait_send()

    @pl.when(across)
    def _():
        for copy in e_copies():
            copy.wait_send()


def put_out(*refs):
    done, refs = refs[:2], refs[2:]
    weights, fields, outs, last, T, sem = refs[:5], refs[5:12], refs[12:14], refs[14:16], refs[16], refs[17]
    depth, rows, _ = done[0].shape
    odd = lax.rem(lax.axis_index("gx"), 2)
    first, part = HALO * (1 - odd), (depth - HALO) // 3
    copies = [
        pltpu.make_async_copy(done[i].at[at], outs[i].at[at], sem.at[i, q])
        for q in range(3) for i in range(2) for at in (pl.ds(first + q * part, part),)
    ]
    for copy in copies:
        copy.start()
    begin = HALO + odd * (depth - HALO)
    own0 = R0 + HALO
    each(begin, HALO, lambda p, j: finish(weights, fields, T, last, p, j, ((own0, rows),)), FINISH)
    at = pl.ds(odd * (depth - HALO), HALO)
    rest = [pltpu.make_async_copy(last[i].at[at], outs[i].at[at], sem.at[i, 3]) for i in range(2)]
    for copy in rest:
        copy.start()
    for copy in copies + rest:
        copy.wait()


def solution(mesh):
    nx, ny = mesh.shape["gx"], mesh.shape["gy"]

    def step(initial, material, goal_faces, conductivity):
        depth, rows, lanes = initial.shape
        planes, tall = depth + 2 * HALO, rows + 2 * HALO + 16
        f32, i32 = jnp.float32, jnp.int32
        by_rows = (depth, rows // HALO, HALO, lanes)
        halos = []
        for shape in ((planes, rows, lanes), (2, planes, HALO, lanes), (HALO, 2 * HALO, lanes)):
            halos += [pltpu.VMEM(shape, t) for t in (f32, i32, i32)]
        sem = pltpu.SemaphoreType.DMA
        whole = pl.BlockSpec(memory_space=pltpu.MemorySpace.HBM)
        inside = pl.BlockSpec(memory_space=pltpu.VMEM)

        def keep(v):
            return pltpu.with_memory_space_constraint(v, pltpu.MemorySpace.HBM)

        args = (conductivity, initial, material, goal_faces,
                initial.reshape(by_rows), material.reshape(by_rows), goal_faces.reshape(by_rows))
        field = pltpu.VMEM((planes, tall, lanes), f32)
        block = pltpu.VMEM(initial.shape, f32)
        made = pl.pallas_call(
            functools.partial(kernel, nx, ny),
            out_shape=[block] * 2 + [field] * 12,
            in_specs=[whole] * 7,
            out_specs=[inside] * 14,
            scratch_shapes=halos
            + [field] * 4
            + [pltpu.VMEM((tall, lanes), f32), pltpu.VMEM((FINISH, 3, tall, lanes), f32)]
            + [pltpu.SMEM(conductivity.shape, f32), sem((4,)), sem((2, 4)), sem((2, 4)),
               sem((2, 3)), sem((2, 3)), sem((2, 2, 3)), sem((2, 2, 3)), sem((3,)), sem((3,)),
               pltpu.SemaphoreType.REGULAR],
            compiler_params=pltpu.CompilerParams(
                collective_id=0, has_side_effects=True, vmem_limit_bytes=30 << 20),
            name="cells",
        )(*(keep(v) for v in args))
        return pl.pallas_call(
            put_out,
            out_shape=[jax.ShapeDtypeStruct(initial.shape, f32)] * 2,
            in_specs=[inside] * 14,
            out_specs=[pl.BlockSpec(memory_space=pl.ANY)] * 2,
            scratch_shapes=[block] * 2 + [pltpu.VMEM((FINISH, 3, tall, lanes), f32), sem((2, 4))],
            compiler_params=pltpu.CompilerParams(vmem_limit_bytes=8 << 20),
            name="put_out",
        )(*made)

    placed = P("gx", "gy", None)
    return jax.shard_map(
        step,
        mesh=mesh,
        in_specs=(placed, placed, placed, P()),
        out_specs=(placed, placed),
        check_vma=False,
    )
```
